32 devices in a mesh: fine: 8 (over y, x, core), coarse: 4 (over z).
Axes of the slice: x: 2, y: 2, z: 4, core: 2. Of those that a mesh axis runs over, the one named last changes fastest.
Arguments:
- force: float32 [3, 131072], P(None, ('fine', 'coarse')), may hold values from -6 to 6
- inv_diag: float32 [3, 131072], P(None, ('fine', 'coarse')), may hold values from 0.01 to 0.03
- k_ref: float32 [24, 24], replicated
- coefs: float32 [65536], P(('fine', 'coarse')), may hold values from 0.5 to 2
- conn: int32 [8, 65536], P(None, ('fine', 'coarse')), may hold values from 0 to 5119
- felem: int32 [24576], P(('fine', 'coarse')), may hold values from 0 to 2047
- weights: float32 [8, 8, 24576], P(None, None, ('fine', 'coarse')), may hold values from -0.6 to 0.6
- counts: int32 [32, 32], P(('fine', 'coarse')), may hold values from 1 to 24, as said below
- celem: int32 [32, 768], P(('fine', 'coarse')), may hold values from 0 to 127
Outputs:
- smoothed: float32 [3, 131072], P(None, ('fine', 'coarse'))
- coarse_load: float32 [24, 4096], P(None, ('fine', 'coarse'))
The draws below stay inside these ranges and needn't reach their ends.
Inputs may be any that keep to these rules, and one draw needn't show every extreme that they name: `counts`: in every draw one owner receives 24 used slots from every partition; every count is at least 1.
All inputs are finite; a program needn't handle non-finite values.
Results may differ from the reference program's by a relative error of at most 0.0003.
Values sent between devices are 32-bit elements; how exact they have to be, the bound alone decides.
A program may use at most 128 MiB of HBM per device.

```python
import math
import jax
import jax.numpy as jnp
from jax import lax

NODE_DEV = 4096
ELEM_DEV = 2048
BAND = 512
CAP = 24
CE_DEV = 128
OWNERS = 32
NODES = 131072
ELEMS = 65536
SLOTS = 24576
CE_ALL = 4096


def draw_k_ref(key, part):
    first = jax.random.fold_in(key, 11)
    second = jax.random.fold_in(key, 12)
    raw = jax.random.uniform(first, (24, 24), jnp.float32, -0.5, 0.5)
    sym = (raw + raw.T) * 0.5
    off = sym * (1.0 - jnp.eye(24, dtype=jnp.float32))
    extra = jax.random.uniform(second, (24,), jnp.float32, 0.5, 1.5)
    return off + jnp.diag(jnp.sum(jnp.abs(off), axis=1) + extra)


def draw_counts(key, part):
    first = jax.random.fold_in(key, 21)
    second = jax.random.fold_in(key, 22)
    third = jax.random.fold_in(key, 23)
    level = jax.random.randint(first, (OWNERS,), CAP // 2, CAP + 1)
    lower = jnp.maximum(level * 3 // 4, 1)
    drawn = jax.random.randint(second, (OWNERS, OWNERS), lower[None, :], level[None, :] + 1)
    busiest = jax.random.randint(third, (), 0, OWNERS)
    column = jnp.arange(OWNERS, dtype=jnp.int32)[None, :]
    return jnp.where(column == busiest, CAP, drawn).astype(jnp.int32)


def place_ends(array, stream_key, low, high):
    index_at = [jax.random.randint(jax.random.fold_in(stream_key, axis), (), 0, length) for axis, length in enumerate(array.shape)]
    main_axis = array.shape.index(max(array.shape))
    next_to = index_at[:main_axis] + [(index_at[main_axis] + 1) % array.shape[main_axis]] + index_at[main_axis + 1:]
    return array.at[tuple(index_at)].set(low).at[tuple(next_to)].set(high)


def levels(rng, shape, pieces, smallest, largest):
    def one(position, parts):
        steps = jax.random.uniform(jax.random.fold_in(jax.random.fold_in(rng, 6), position), (parts,), jnp.float32, smallest / len(pieces), largest / len(pieces))
        return jnp.repeat(jnp.exp(steps), shape[position] // parts).reshape((-1,) + (1,) * (len(shape) - position - 1))

    factor_of = one(*pieces[0])
    for cut in pieces[1:]:
        factor_of = factor_of * one(*cut)
    return factor_of


def centred(own_key, dims, width, most, cuts=(), kind=jnp.bfloat16):
    level = levels(own_key, dims, cuts, -0.22, 0.18) if cuts else 1.0
    entries = jax.random.normal(own_key, dims, jnp.float32) * width * level
    return jnp.minimum(jnp.maximum(entries, -most), most).astype(kind)


def setup_inputs(seed: int = 0) -> dict:
    streams_of = jax.random.split(jax.random.key(seed), 10)
    return {
        "force": centred(streams_of[0], (3, NODES), 1.0, 6.0, ((1, 32),), jnp.float32),
        "inv_diag": jnp.clip(jnp.exp(math.log(0.03) - 1.0986123 * jax.random.uniform(streams_of[1], (3, NODES), jnp.float32) ** levels(streams_of[1], (3, NODES), ((1, 32),), -0.2, 0.2)), 0.01, 0.03),
        "k_ref": draw_k_ref(jax.random.fold_in(streams_of[9], 71), 0),
        "coefs": jnp.clip(jnp.exp(math.log(2.0) - 1.3862944 * jax.random.uniform(streams_of[3], (ELEMS,), jnp.float32) ** levels(streams_of[3], (ELEMS,), ((0, 32),), -0.2, 0.2)), 0.5, 2.0),
        "conn": place_ends(jax.random.randint(streams_of[4], (8, ELEMS), 0, NODE_DEV + 2 * BAND), jax.random.fold_in(streams_of[4], 1), 0, (NODE_DEV + 2 * BAND) - 1).astype(jnp.int32),
        "felem": place_ends(jax.random.randint(streams_of[5], (SLOTS,), 0, ELEM_DEV), jax.random.fold_in(streams_of[5], 1), 0, ELEM_DEV - 1).astype(jnp.int32),
        "weights": centred(streams_of[6], (8, 8, SLOTS), 0.1, 0.6, ((2, 32),), jnp.float32),
        "counts": draw_counts(jax.random.fold_in(streams_of[9], 71), 0),
        "celem": place_ends(jax.random.randint(streams_of[8], (OWNERS, OWNERS * CAP), 0, CE_DEV), jax.random.fold_in(streams_of[8], 1), 0, CE_DEV - 1).astype(jnp.int32),
    }


LOW_END = 0.3
HIGH_END = 2.5


def apply_operator(field, k_ref, coefs, index):
    padded = jnp.pad(field, ((0, 0), (BAND, BAND)))
    local = padded[:, index].reshape(24, -1)
    product = jnp.dot(k_ref, local, precision=lax.Precision.HIGHEST, preferred_element_type=jnp.float32) * coefs[None, :]
    summed = jnp.zeros(padded.shape, jnp.float32).at[:, index].add(product.reshape(3, 8, -1))
    return summed[:, BAND:-BAND]


def reference(force, inv_diag, k_ref, coefs, conn, felem, weights, counts, celem):
    offset = (jnp.arange(ELEMS, dtype=jnp.int32) // ELEM_DEV) * NODE_DEV
    index = conn + offset[None, :]
    theta = (HIGH_END + LOW_END) / 2.0
    delta = (HIGH_END - LOW_END) / 2.0
    sigma = theta / delta
    rho = 1.0 / sigma
    solution = jnp.zeros_like(force)
    resid = force
    direction = inv_diag * resid / theta
    for sweep in range(3):
        solution = solution + direction
        resid = resid - apply_operator(direction, k_ref, coefs, index)
        if sweep < 2:
            rho_new = 1.0 / (2.0 * sigma - rho)
            direction = rho_new * rho * direction + (2.0 * rho_new / delta) * inv_diag * resid
            rho = rho_new
    padded_r = jnp.pad(resid, ((0, 0), (BAND, BAND)))
    per_src = OWNERS * CAP
    felem_blocks = felem.reshape(OWNERS, per_src)
    weight_blocks = jnp.transpose(weights.reshape(8, 8, OWNERS, per_src), (2, 0, 1, 3))
    slot_iota = jnp.arange(per_src, dtype=jnp.int32)

    def one_source(packed):
        source, fine_ids, block_w, count_row = packed
        elem_ids = fine_ids + source * ELEM_DEV
        node_ids = conn[:, elem_ids] + source * NODE_DEV
        values = padded_r[:, node_ids]
        contrib = jnp.einsum("ijs,cjs->cis", block_w, values, precision=lax.Precision.HIGHEST)
        live = (slot_iota % CAP) < count_row[slot_iota // CAP]
        return (contrib * live[None, None, :].astype(jnp.float32)).reshape(24, per_src)

    sources = jnp.arange(OWNERS, dtype=jnp.int32)
    contribs = lax.map(one_source, (sources, felem_blocks, weight_blocks, counts))
    data = jnp.transpose(contribs.reshape(OWNERS, 24, OWNERS, CAP), (0, 2, 3, 1)).reshape(-1, 24)
    owner_ids = jnp.transpose(celem.reshape(OWNERS, OWNERS, CAP), (1, 0, 2))
    owner_ids = owner_ids + (jnp.arange(OWNERS, dtype=jnp.int32) * CE_DEV)[None, :, None]
    load = jax.ops.segment_sum(data, owner_ids.reshape(-1), num_segments=CE_ALL)
    return solution, load.T
```

```python
import functools

import jax
import jax.numpy as jnp
from jax import lax
from jax.experimental import pallas as pl
from jax.experimental.pallas import tpu as pltpu
from jax.sharding import PartitionSpec as P

BAND = 512
CAP = 24
CE_DEV = 128
LOW_END = 0.3
HIGH_END = 2.5
SWEEPS = 3
LANES = 128
ROW = 256
SPACE = 32
TERMS = 3
STEP = 16.0
TOP = 256.0
TINY = 1e-36
BLOCK = 16
PAD = 96
F8 = jnp.float8_e4m3fn
GROUP = 16
TILES = 2

THETA = (HIGH_END + LOW_END) / 2.0
DELTA = (HIGH_END - LOW_END) / 2.0
SIGMA = THETA / DELTA


def schedule():
    rho = 1.0 / SIGMA
    steps = []
    for _ in range(SWEEPS - 1):
        rho_new = 1.0 / (2.0 * SIGMA - rho)
        steps.append((rho_new * rho, 2.0 * rho_new / DELTA))
        rho = rho_new
    return steps + [(0.0, 0.0)]


def split(value):
    high = value.astype(jnp.bfloat16).astype(jnp.float32)
    return (high, value - high)


def terms(value):
    out = []
    for _ in range(TERMS):
        part = value.astype(F8).astype(jnp.float32)
        out.append(part)
        value = (value - part) * STEP
    return out


def largest(value):
    return jnp.max(jnp.abs(value), axis=(0, 1), keepdims=True)


def joined(parts):
    out = parts[-1]
    for part in parts[-2::-1]:
        out = part + out * (1.0 / STEP)
    return out


def pick(row, index):
    table = jnp.broadcast_to(row, index.shape)
    return jnp.take_along_axis(table, index, axis=1, mode="promise_in_bounds")


def spread(tiles, lane, local):
    first, at = divmod(local * CAP, LANES)
    out = None
    for c, row in enumerate(tiles):
        piece = pltpu.roll(row[first], (c * SPACE - at) % LANES, axis=1)
        left = LANES - at
        if left < CAP:
            rest = pltpu.roll(row[first + 1], (c * SPACE + left) % LANES, axis=1)
            piece = jnp.where(lane < c * SPACE + left, piece, rest)
        out = piece if c == 0 else jnp.where(lane < c * SPACE, out, piece)
    return out


def kernel(
    sizes, force_in, inv_diag_in, k_ref_in, coefs_in, conn_in, felem_in, weights_in, counts,
    celem_in, smoothed, load,
    force, inv_diag, k_ref, coefs, conn, felem, weights, celem,
    direction, resid, scale, total, local, force_e, split_f, outer_row, inner_row, onehot,
    onehot_t, table_a, table_b, picked, spread_k, slot_node, values, contrib,
    sent, selector, arrived, stacked, snd, rcv,
    snd_sem, rcv_sem, out_sem, in_sem, own_sem, load_sem,
):
    fine, coarse = sizes
    devices = fine * coarse
    me = lax.axis_index("fine") * coarse + lax.axis_index("coarse")
    nodes = force.shape[1]
    owned = nodes // ROW
    edge = BAND // ROW
    rows = owned + 2 * edge
    stride = total.shape[0] // 3
    elems = conn.shape[1]
    slots = felem.shape[1]
    window = 2 * edge

    half = snd.shape[2] // 2

    def put_edge(phase, d, to, value):
        count = value.shape[0]
        snd[phase, d, to : to + count, :] = value[:, :LANES]
        snd[phase, d, half + to : half + to + count, :] = value[:, LANES:]

    def get_edge(phase, d, to, count):
        return jnp.concatenate(
            [rcv[phase, d, at : at + count, :] for at in (to, half + to)], axis=1
        )

    def place(index):
        return (index // coarse, lax.rem(index, coarse))

    pairs = [
        (force_in, force), (inv_diag_in, inv_diag), (conn_in, conn), (felem_in, felem.at[0]),
        (celem_in, celem), (k_ref_in, k_ref), (coefs_in, coefs.at[0]), (weights_in, weights),
    ]
    loads = [pltpu.make_async_copy(a, b, load_sem.at[n]) for n, (a, b) in enumerate(pairs)]
    for copy in loads:
        copy.start()

    barrier = pltpu.get_barrier_semaphore()

    @pl.loop(1, devices)
    def _(step):
        pl.semaphore_signal(
            barrier, inc=1, device_id=place(lax.rem(me + step, devices)),
            device_id_type=pl.DeviceIdType.MESH,
        )

    resid[...] = jnp.zeros_like(resid)
    scale[...] = jnp.zeros_like(scale)
    loads[0].wait()
    loads[1].wait()
    for c in range(3):
        for h in range(owned):
            at = c * stride + edge + h
            resid[at : at + 1, :] = force[c : c + 1, h * ROW : (h + 1) * ROW]
            scale[at : at + 1, :] = inv_diag[c : c + 1, h * ROW : (h + 1) * ROW]
    for d, begin in enumerate((edge, owned)):
        for a, field in enumerate((resid, scale)):
            for c in range(3):
                at = c * stride + begin
                to = (a * 3 + c) * edge
                put_edge(0, d, to, field[at : at + edge, :])

    for copy in loads[2:5]:
        copy.wait()

    pl.semaphore_wait(barrier, devices - 1)

    lower, upper = (place(lax.rem(me + devices - 1, devices)), place(lax.rem(me + 1, devices)))

    def edge_copy(phase, d, target):
        return pltpu.make_async_remote_copy(
            src_ref=snd.at[phase, d],
            dst_ref=rcv.at[phase, d],
            send_sem=snd_sem.at[phase, d],
            recv_sem=rcv_sem.at[phase, d],
            device_id=target,
            device_id_type=pl.DeviceIdType.MESH,
        )

    def edge_start(phase):
        down, up = edge_copy(phase, 0, lower), edge_copy(phase, 1, upper)

        @pl.when(me > 0)
        def _():
            down.start()

        @pl.when(me < devices - 1)
        def _():
            up.start()

    def edge_wait(phase):
        down, up = edge_copy(phase, 0, lower), edge_copy(phase, 1, upper)

        @pl.when(me > 0)
        def _():
            up.wait_recv()
            down.wait_send()

        @pl.when(me < devices - 1)
        def _():
            down.wait_recv()
            up.wait_send()

    edge_start(0)

    span = window * 2
    node_row = lax.shift_right_logical(conn[...], 8)
    outer_row[...] = jnp.where(
        node_row < window, node_row, jnp.where(node_row < owned, span, node_row - owned + window)
    )
    inner_row[...] = node_row - window

    def as_bf16(index):
        return index.astype(jnp.float32).astype(jnp.bfloat16)

    one, none = jnp.bfloat16(1.0), jnp.bfloat16(0.0)

    @pl.loop(0, 8)
    def _(j):
        low = as_bf16(jnp.bitwise_and(conn[pl.ds(j, 1), :], ROW - 1))
        hit = as_bf16(lax.broadcasted_iota(jnp.int32, (ROW, elems), 0)) == low
        onehot[j] = jnp.where(hit, one, none).astype(F8)

    for t in range(elems // LANES):
        turned = jnp.transpose(
            jnp.bitwise_and(conn[:, t * LANES : (t + 1) * LANES], ROW - 1).astype(jnp.float32)
        )
        along = as_bf16(lax.broadcasted_iota(jnp.int32, (LANES, ROW), 1))
        for j in range(8):
            low = jnp.broadcast_to(turned[:, j : j + 1], (LANES, ROW)).astype(jnp.bfloat16)
            onehot_t[j, t * LANES : (t + 1) * LANES, :] = jnp.where(along == low, one, none).astype(F8)

    @pl.loop(0, slots // LANES, unroll=2)
    def _(tile):
        at = pl.multiple_of(tile * LANES, LANES)
        element = jnp.broadcast_to(felem[:, pl.ds(at, LANES)], (8, LANES))
        low = jnp.bitwise_and(element, LANES - 1)
        high = lax.shift_right_logical(element, 7)
        found = jnp.zeros((8, LANES), jnp.int32)
        for t in range(elems // LANES):
            got = jnp.take_along_axis(
                conn[:, t * LANES : (t + 1) * LANES], low, axis=1, mode="promise_in_bounds"
            )
            found = jnp.where(high == t, got, found)
        slot_node[:, pl.ds(at, LANES)] = found

    lane = lax.broadcasted_iota(jnp.int32, (8, LANES), 1)
    coarse_iota = lax.broadcasted_iota(jnp.int32, (CE_DEV, LANES), 0)
    group_tiles = GROUP * CAP // LANES

    @pl.loop(0, devices // GROUP)
    def _(group):
        base = group * (GROUP * CAP)
        ids = [
            jnp.broadcast_to(
                celem[:, pl.ds(pl.multiple_of(base + t * LANES, LANES), LANES)], (8, LANES)
            )
            for t in range(group_tiles)
        ]
        for o in range(GROUP):
            owner = spread([ids, ids, ids], lane, o)
            hit = coarse_iota == owner[0:1, :]
            at = pl.multiple_of((group * GROUP + o) * LANES, LANES)
            selector[:, pl.ds(at, LANES)] = jnp.where(hit, 1.0, 0.0).astype(jnp.bfloat16)

    for copy in loads[5:]:
        copy.wait()

    k_all = k_ref[...]
    reach = largest(jnp.sum(jnp.abs(k_all), axis=1, keepdims=True)) * largest(coefs[...])
    column = lax.broadcasted_iota(jnp.int32, (24, 8 * BLOCK), 1)
    which_q = jnp.minimum(jnp.bitwise_and(column, BLOCK - 1), 3 * TERMS - 1)
    which_s = lax.shift_right_logical(which_q * 11, 5)
    dof = (which_q - which_s * 3) * 8 + lax.shift_right_logical(column, 4)
    same = lax.broadcasted_iota(jnp.int32, (24, 8 * BLOCK), 0) == dof
    share = jnp.where(which_s == 0, 1.0, jnp.where(which_s == 1, 1.0 / STEP, 1.0 / STEP**2))
    spread_k[...] = jnp.dot(
        jnp.concatenate(split(k_all), axis=0), jnp.where(same, share, 0.0),
        precision=lax.Precision.HIGHEST, preferred_element_type=jnp.float32,
    ).astype(jnp.bfloat16)

    def fill_edges():
        @pl.when(me > 0)
        def _():
            for a, field in enumerate((resid, scale)):
                for c in range(3):
                    at, to = (c * stride, (a * 3 + c) * edge)
                    field[at : at + edge, :] = get_edge(0, 1, to, edge)

        @pl.when(me < devices - 1)
        def _():
            for a, field in enumerate((resid, scale)):
                for c in range(3):
                    at, to = (c * stride + edge + owned, (a * 3 + c) * edge)
                    field[at : at + edge, :] = get_edge(0, 0, to, edge)

        direction[...] = scale[...] * resid[...] / THETA

    def add_edges(phase, add):
        def from_side(d, begin):
            for c in range(3):
                at = slice(c * stride + begin, c * stride + begin + window)
                theirs = get_edge(phase, d, c * window, window)
                resid[at, :] -= theirs
                direction[at, :] -= add * scale[at, :] * theirs

        def clear(begin):
            for c in range(3):
                at = c * stride + begin
                resid[at : at + edge, :] = jnp.zeros((edge, ROW), jnp.float32)

        @pl.when(me > 0)
        def _():
            from_side(1, 0)

        @pl.when(me == 0)
        def _():
            clear(0)

        @pl.when(me < devices - 1)
        def _():
            from_side(0, owned)

        @pl.when(me == devices - 1)
        def _():
            clear(edge + owned)

    tables = (table_a, table_b)
    for side in tables:
        side[...] = jnp.zeros_like(side)
    direction[...] = scale[...] * resid[...] / THETA
    total[...] = jnp.zeros_like(total)

    per_row = ROW // LANES
    inner = range(window * per_row, owned * per_row)
    outer = [h for h in range(rows * per_row) if h not in inner]

    def gather(field, index, hs, out):
        low = [jnp.bitwise_and(i, LANES - 1) for i in index]
        high = [lax.shift_right_logical(i, 7) for i in index]
        for h in hs:
            at, side = divmod(h, per_row)
            here = [i == h for i in high]
            for c in range(3):
                r = c * stride + at
                row = field[r : r + 1, side * LANES : (side + 1) * LANES]
                for t in range(len(index)):
                    out[c][t] = jnp.where(here[t], pick(row, low[t]), out[c][t])
        return out

    def gather_local(hs, first):
        @pl.loop(0, elems // (LANES * TILES))
        def _(chunk):
            starts = [pl.multiple_of((chunk * TILES + t) * LANES, LANES) for t in range(TILES)]
            index = [conn[:, pl.ds(s, LANES)] for s in starts]
            out = [
                [
                    jnp.zeros((8, LANES), jnp.float32)
                    if first
                    else local[c * 8 : (c + 1) * 8, pl.ds(starts[t], LANES)]
                    for t in range(TILES)
                ]
                for c in range(3)
            ]
            got = gather(direction, index, hs, out)
            for c in range(3):
                for t in range(TILES):
                    local[c * 8 : (c + 1) * 8, pl.ds(starts[t], LANES)] = got[c][t]

    steps = schedule()

    def outer_of(field, c):
        low, high = (slice(c * stride + at, c * stride + at + window) for at in (0, owned))
        return jnp.concatenate([field[low, :], field[high, :]], axis=0)

    def inner_of(field):
        return [field[c * stride + window : c * stride + owned, :] for c in range(3)]

    def scatter(rows_of, count):
        iota = lax.broadcasted_iota(jnp.int32, (count, elems), 0)
        height = 3 * TERMS * count
        empty = [jnp.zeros((-height % 32, elems), jnp.float32)] if height % 32 else []
        got = None
        for j in range(8):
            hit = iota == rows_of[j : j + 1, :]
            left = jnp.concatenate(
                [
                    jnp.where(hit, split_f[s * 24 + c * 8 + j : s * 24 + c * 8 + j + 1, :], 0.0)
                    for s in range(TERMS)
                    for c in range(3)
                ]
                + empty,
                axis=0,
            ).astype(F8)
            more = jnp.dot(left, onehot_t[j], preferred_element_type=jnp.float32)
            got = more if got is None else got + more
        return [
            joined([got[(s * 3 + c) * count : (s * 3 + c + 1) * count, :] for s in range(TERMS)])
            for c in range(3)
        ]

    @pl.loop(0, SWEEPS)
    def _(sweep):
        gather_local(inner, True)
        force_e[...] = jnp.dot(
            k_ref[...], local[...], precision=lax.Precision.HIGHEST,
            preferred_element_type=jnp.float32,
        )
        top_inner = functools.reduce(jnp.maximum, [largest(v) for v in inner_of(direction)])
        edge_wait(sweep)

        @pl.when(sweep == 0)
        def _():
            fill_edges()

        @pl.when(sweep > 0)
        def _():
            add_edges(sweep, jnp.where(sweep == 1, steps[0][1], steps[1][1]))

        ends = [outer_of(direction, c) for c in range(3)]
        top = largest(functools.reduce(jnp.maximum, [jnp.abs(v) for v in ends]))
        held = [terms(v * (TOP / jnp.maximum(top, TINY))) for v in ends]
        for t, side in enumerate(tables):
            lanes = slice(t * LANES, (t + 1) * LANES)
            for q in range(8):
                side[pl.ds(q, span, stride=8), :] = held[q % 3][q // 3][:, lanes]
            side[8 * span : 9 * span, :] = held[2][2][:, lanes]
        nodes8 = jnp.concatenate([side[...] for side in tables], axis=1).astype(F8)
        iota = lax.broadcasted_iota(jnp.int32, (span, elems), 0)
        for j in range(8):
            row = jnp.broadcast_to(outer_row[j : j + 1, :], (8, elems))
            found = jnp.dot(nodes8, onehot[j], preferred_element_type=jnp.float32)
            first = jnp.zeros((8, elems), jnp.float32)
            for h in range(span):
                first = jnp.where(row == h, found[h * 8 : (h + 1) * 8, :], first)
            last = jnp.where(row == iota, found[8 * span : 9 * span, :], 0.0)
            picked[j * BLOCK : (j + 1) * BLOCK, :] = jnp.concatenate([first, last], axis=0).astype(
                jnp.bfloat16
            )
        moved = jnp.dot(spread_k[...], picked[...], preferred_element_type=jnp.float32)
        moved = moved[:24, :] + moved[24:, :]
        bound = jnp.maximum(reach * jnp.maximum(top, top_inner), TINY)
        forces = (force_e[...] + moved * (top * (1.0 / TOP))) * coefs[...]
        for s, v in enumerate(terms(forces * (TOP / bound))):
            split_f[s * 24 : (s + 1) * 24, :] = v

        unit = bound * (1.0 / TOP)
        keep = jnp.where(sweep == 0, steps[0][0], steps[1][0])
        add = jnp.where(sweep == 0, steps[0][1], steps[1][1])
        given = [v * unit for v in scatter(outer_row, span)]
        for d in range(2):
            for c in range(3):
                put_edge(sweep + 1, d, c * window, given[c][d * window : (d + 1) * window, :])
        edge_start(sweep + 1)
        total[...] += direction[...]

        def update(at, value):
            new = resid[at, :] - value
            resid[at, :] = new
            direction[at, :] = keep * direction[at, :] + add * scale[at, :] * new

        for c in range(3):
            for d, begin in enumerate((0, owned)):
                update(
                    slice(c * stride + begin, c * stride + begin + window),
                    given[c][d * window : (d + 1) * window, :],
                )
        middle = owned - window
        given = scatter(inner_row, -(-middle // 8) * 8)
        for c in range(3):
            update(slice(c * stride + window, c * stride + owned), given[c][:middle, :] * unit)

    @pl.loop(0, slots // LANES, unroll=2)
    def _(tile):
        at = pl.multiple_of(tile * LANES, LANES)
        begun = [[jnp.zeros((8, LANES), jnp.float32)] for _ in range(3)]
        got = gather(resid, [slot_node[:, pl.ds(at, LANES)]], inner, begun)
        for c in range(3):
            contrib[c * 8 : (c + 1) * 8, pl.ds(at, LANES)] = got[c][0]

    edge_wait(SWEEPS)
    add_edges(SWEEPS, 0.0)

    @pl.loop(0, slots // LANES, unroll=2)
    def _(tile):
        at = pl.multiple_of(tile * LANES, LANES)
        begun = [[contrib[c * 8 : (c + 1) * 8, pl.ds(at, LANES)]] for c in range(3)]
        got = gather(resid, [slot_node[:, pl.ds(at, LANES)]], outer, begun)
        for c in range(3):
            values[c * 8 : (c + 1) * 8, :] = got[c][0]
        for c in range(3):
            acc = jnp.zeros((8, LANES), jnp.float32)
            for j in range(8):
                acc = acc + weights[:, j, pl.ds(at, LANES)] * values[c * 8 + j : c * 8 + j + 1, :]
            contrib[c * 8 : (c + 1) * 8, pl.ds(at, LANES)] = acc

    lane_slot = jnp.bitwise_and(lane, SPACE - 1)

    @pl.loop(0, devices // GROUP)
    def _(group):
        base = group * (GROUP * CAP)
        tiles = [
            [
                contrib[
                    c * 8 : (c + 1) * 8,
                    pl.ds(pl.multiple_of(base + t * LANES, LANES), LANES),
                ]
                for t in range(group_tiles)
            ]
            for c in range(3)
        ]
        for o in range(GROUP):
            owner = group * GROUP + o
            live = (lane_slot < counts[0, owner]) & (lane < 3 * SPACE)
            sent[owner] = jnp.where(live, spread(tiles, lane, o), 0.0)

    def slot_copy(target):
        return pltpu.make_async_remote_copy(
            src_ref=sent.at[target],
            dst_ref=arrived.at[me],
            send_sem=out_sem.at[target],
            recv_sem=in_sem.at[me],
            device_id=place(target),
            device_id_type=pl.DeviceIdType.MESH,
        )

    def slot_arrival(source):
        return pltpu.make_async_remote_copy(
            src_ref=sent.at[source],
            dst_ref=arrived.at[source],
            send_sem=out_sem.at[source],
            recv_sem=in_sem.at[source],
            device_id=place(source),
            device_id_type=pl.DeviceIdType.MESH,
        )

    @pl.loop(1, devices)
    def _(step):
        slot_copy(lax.rem(me + step, devices)).start()

    own = pltpu.make_async_copy(sent.at[me], arrived.at[me], own_sem)
    own.start()

    for c in range(3):
        for h in range(owned):
            at = c * stride + edge + h
            smoothed[c : c + 1, h * ROW : (h + 1) * ROW] = total[at : at + 1, :]

    own.wait()

    @pl.loop(1, devices)
    def _(step):
        slot_arrival(lax.rem(me + step, devices)).wait_recv()

    @pl.loop(0, devices)
    def _(source):
        got = arrived[source]
        pieces = [
            split(jnp.where((lane >= c * SPACE) & (lane < (c + 1) * SPACE), got, 0.0))
            for c in range(3)
        ]
        stacked[:, pl.ds(pl.multiple_of(source * LANES, LANES), LANES)] = jnp.concatenate(
            [pieces[c][s] for s in range(2) for c in range(3)], axis=0
        ).astype(jnp.bfloat16)

    sums = lax.dot_general(
        stacked[...], selector[...], (((1,), (1,)), ((), ())), preferred_element_type=jnp.float32
    )
    load[...] = sums[:24, :] + sums[24:, :]

    @pl.loop(1, devices)
    def _(step):
        slot_copy(lax.rem(me + step, devices)).wait_send()


def on_device(sizes, force, inv_diag, k_ref, coefs, conn, felem, weights, counts, celem):
    devices = sizes[0] * sizes[1]
    nodes = force.shape[1]
    elems = conn.shape[1]
    slots = felem.shape[0]
    rows = (nodes + 2 * BAND) // ROW
    stride = -(-rows // 8) * 8
    edge_rows = 6 * BAND // ROW
    field = pltpu.VMEM((3 * stride, ROW), jnp.float32)
    edges = pltpu.VMEM((SWEEPS + 1, 2, edge_rows * ROW // LANES, LANES), jnp.float32)
    vmem = pl.BlockSpec(memory_space=pltpu.VMEM)
    hbm = pl.BlockSpec(memory_space=pltpu.HBM)
    smem = pl.BlockSpec(memory_space=pltpu.SMEM)
    return pl.pallas_call(
        functools.partial(kernel, sizes),
        out_shape=(
            jax.ShapeDtypeStruct((3, nodes), jnp.float32),
            jax.ShapeDtypeStruct((24, CE_DEV), jnp.float32),
        ),
        in_specs=[hbm] * 7 + [smem, hbm],
        out_specs=(vmem, vmem),
        scratch_shapes=[
            pltpu.VMEM((3, nodes), jnp.float32),
            pltpu.VMEM((3, nodes), jnp.float32),
            pltpu.VMEM((24, 24), jnp.float32),
            pltpu.VMEM((1, elems), jnp.float32),
            pltpu.VMEM((8, elems), jnp.int32),
            pltpu.VMEM((1, slots), jnp.int32),
            pltpu.VMEM((8, 8, slots), jnp.float32),
            pltpu.VMEM((1, slots), jnp.int32),
            field,
            field,
            field,
            field,
            pltpu.VMEM((24, elems), jnp.float32),
            pltpu.VMEM((24, elems), jnp.float32),
            pltpu.VMEM((24 * TERMS, elems), jnp.float32),
            pltpu.VMEM((8, elems), jnp.int32),
            pltpu.VMEM((8, elems), jnp.int32),
            pltpu.VMEM((8, ROW, elems), F8),
            pltpu.VMEM((8, elems, ROW), F8),
            pltpu.VMEM((PAD, LANES), jnp.float32),
            pltpu.VMEM((PAD, LANES), jnp.float32),
            pltpu.VMEM((8 * BLOCK, elems), jnp.bfloat16),
            pltpu.VMEM((48, 8 * BLOCK), jnp.bfloat16),
            pltpu.VMEM((8, slots), jnp.int32),
            pltpu.VMEM((24, LANES), jnp.float32),
            pltpu.VMEM((24, slots), jnp.float32),
            pltpu.VMEM((devices, 8, LANES), jnp.float32),
            pltpu.VMEM((CE_DEV, devices * LANES), jnp.bfloat16),
            pltpu.VMEM((devices, 8, LANES), jnp.float32),
            pltpu.VMEM((48, devices * LANES), jnp.bfloat16),
            edges,
            edges,
            pltpu.SemaphoreType.DMA((SWEEPS + 1, 2)),
            pltpu.SemaphoreType.DMA((SWEEPS + 1, 2)),
            pltpu.SemaphoreType.DMA((devices,)),
            pltpu.SemaphoreType.DMA((devices,)),
            pltpu.SemaphoreType.DMA,
            pltpu.SemaphoreType.DMA((8,)),
        ],
        compiler_params=pltpu.CompilerParams(
            collective_id=0, has_side_effects=True, vmem_limit_bytes=64 * 1024 * 1024
        ),
    )(force, inv_diag, k_ref, coefs, conn, felem, weights, counts, celem)


def solution(mesh):
    both = ("fine", "coarse")
    placed = (
        P(None, both),
        P(None, both),
        P(),
        P(both),
        P(None, both),
        P(both),
        P(None, None, both),
        P(both, None),
        P(both, None),
    )
    sizes = (mesh.shape["fine"], mesh.shape["coarse"])
    return jax.shard_map(
        functools.partial(on_device, sizes),
        mesh=mesh,
        in_specs=placed,
        out_specs=(P(None, both), P(None, both)),
        check_vma=False,
    )
```

```python
import functools

import jax
import jax.numpy as jnp
from jax import lax
from jax.experimental import pallas as pl
from jax.experimental.pallas import tpu as pltpu
from jax.sharding import PartitionSpec as P

BAND = 512
CAP = 24
CE_DEV = 128
LOW_END = 0.3
HIGH_END = 2.5
SWEEPS = 3
LANES = 128
ROW = 256
SPACE = 32
TERMS = 3
STEP = 16.0
TOP = 256.0
TINY = 1e-36
BLOCK = 16
PAD = 96
F8 = jnp.float8_e4m3fn
GROUP = 16
TILES = 2

THETA = (HIGH_END + LOW_END) / 2.0
DELTA = (HIGH_END - LOW_END) / 2.0
SIGMA = THETA / DELTA


def schedule():
    rho = 1.0 / SIGMA
    steps = []
    for _ in range(SWEEPS - 1):
        rho_new = 1.0 / (2.0 * SIGMA - rho)
        steps.append((rho_new * rho, 2.0 * rho_new / DELTA))
        rho = rho_new
    return steps + [(0.0, 0.0)]


def split(value):
    high = value.astype(jnp.bfloat16).astype(jnp.float32)
    return (high, value - high)


def terms(value):
    out = []
    for _ in range(TERMS):
        part = value.astype(F8).astype(jnp.float32)
        out.append(part)
        value = (value - part) * STEP
    return out


def largest(value):
    return jnp.max(jnp.abs(value), axis=(0, 1), keepdims=True)


def joined(parts):
    out = parts[-1]
    for part in parts[-2::-1]:
        out = part + out * (1.0 / STEP)
    return out


def pick(row, index):
    table = jnp.broadcast_to(row, index.shape)
    return jnp.take_along_axis(table, index, axis=1, mode="promise_in_bounds")


def spread(tiles, lane, local):
    first, at = divmod(local * CAP, LANES)
    out = None
    for c, row in enumerate(tiles):
        piece = pltpu.roll(row[first], (c * SPACE - at) % LANES, axis=1)
        left = LANES - at
        if left < CAP:
            rest = pltpu.roll(row[first + 1], (c * SPACE + left) % LANES, axis=1)
            piece = jnp.where(lane < c * SPACE + left, piece, rest)
        out = piece if c == 0 else jnp.where(lane < c * SPACE, out, piece)
    return out


def kernel(
    sizes, force_in, inv_diag_in, k_ref_in, coefs_in, conn_in, felem_in, weights_in, counts_in,
    celem_in, smoothed, load,
    force, inv_diag, k_ref, coefs, conn, felem, weights, celem, counts,
    direction, resid, scale, total, local, force_e, split_f, outer_row, inner_row, onehot,
    onehot_t, table_a, table_b, picked, spread_k, slot_node, values, contrib,
    sent, selector, arrived, stacked, snd, rcv,
    snd_sem, rcv_sem, out_sem, in_sem, own_sem, load_sem,
):
    fine, coarse = sizes
    devices = fine * coarse
    me = lax.axis_index("fine") * coarse + lax.axis_index("coarse")
    nodes = force.shape[1]
    owned = nodes // ROW
    edge = BAND // ROW
    rows = owned + 2 * edge
    stride = total.shape[0] // 3
    elems = conn.shape[1]
    slots = felem.shape[1]
    window = 2 * edge

    half = snd.shape[2] // 2

    def put_edge(phase, d, to, value):
        count = value.shape[0]
        snd[phase, d, to : to + count, :] = value[:, :LANES]
        snd[phase, d, half + to : half + to + count, :] = value[:, LANES:]

    def get_edge(phase, d, to, count):
        return jnp.concatenate(
            [rcv[phase, d, at : at + count, :] for at in (to, half + to)], axis=1
        )

    def place(index):
        return (index // coarse, lax.rem(index, coarse))

    pairs = [
        (force_in, force), (inv_diag_in, inv_diag), (conn_in, conn), (felem_in, felem.at[0]),
        (celem_in, celem), (k_ref_in, k_ref), (coefs_in, coefs.at[0]), (weights_in, weights),
        (counts_in, counts),
    ]
    loads = [pltpu.make_async_copy(a, b, load_sem.at[n]) for n, (a, b) in enumerate(pairs)]
    for copy in loads:
        copy.start()

    barrier = pltpu.get_barrier_semaphore()

    @pl.loop(1, devices)
    def _(step):
        pl.semaphore_signal(
            barrier, inc=1, device_id=place(lax.rem(me + step, devices)),
            device_id_type=pl.DeviceIdType.MESH,
        )

    resid[...] = jnp.zeros_like(resid)
    scale[...] = jnp.zeros_like(scale)
    loads[0].wait()
    loads[1].wait()
    for c in range(3):
        for h in range(owned):
            at = c * stride + edge + h
            resid[at : at + 1, :] = force[c : c + 1, h * ROW : (h + 1) * ROW]
            scale[at : at + 1, :] = inv_diag[c : c + 1, h * ROW : (h + 1) * ROW]
    for d, begin in enumerate((edge, owned)):
        for a, field in enumerate((resid, scale)):
            for c in range(3):
                at = c * stride + begin
                to = (a * 3 + c) * edge
                put_edge(0, d, to, field[at : at + edge, :])

    for copy in loads[2:5]:
        copy.wait()

    span = window * 2
    node_row = lax.shift_right_logical(conn[...], 8)
    outer_row[...] = jnp.where(
        node_row < window, node_row, jnp.where(node_row < owned, span, node_row - owned + window)
    )
    inner_row[...] = node_row - window

    def as_bf16(index):
        return index.astype(jnp.float32).astype(jnp.bfloat16)

    one, none = jnp.bfloat16(1.0), jnp.bfloat16(0.0)

    @pl.loop(0, 8)
    def _(j):
        low = as_bf16(jnp.bitwise_and(conn[pl.ds(j, 1), :], ROW - 1))
        hit = as_bf16(lax.broadcasted_iota(jnp.int32, (ROW, elems), 0)) == low
        onehot[j] = jnp.where(hit, one, none).astype(F8)

    for t in range(elems // LANES):
        turned = jnp.transpose(
            jnp.bitwise_and(conn[:, t * LANES : (t + 1) * LANES], ROW - 1).astype(jnp.float32)
        )
        along = as_bf16(lax.broadcasted_iota(jnp.int32, (LANES, ROW), 1))
        for j in range(8):
            low = jnp.broadcast_to(turned[:, j : j + 1], (LANES, ROW)).astype(jnp.bfloat16)
            onehot_t[j, t * LANES : (t + 1) * LANES, :] = jnp.where(along == low, one, none).astype(F8)

    for copy in loads[5:]:
        copy.wait()

    k_all = k_ref[...]
    reach = largest(jnp.sum(jnp.abs(k_all), axis=1, keepdims=True)) * largest(coefs[...])
    column = lax.broadcasted_iota(jnp.int32, (24, 8 * BLOCK), 1)
    which_q = jnp.minimum(jnp.bitwise_and(column, BLOCK - 1), 3 * TERMS - 1)
    which_s = lax.shift_right_logical(which_q * 11, 5)
    dof = (which_q - which_s * 3) * 8 + lax.shift_right_logical(column, 4)
    same = lax.broadcasted_iota(jnp.int32, (24, 8 * BLOCK), 0) == dof
    share = jnp.where(which_s == 0, 1.0, jnp.where(which_s == 1, 1.0 / STEP, 1.0 / STEP**2))
    spread_k[...] = jnp.dot(
        jnp.concatenate(split(k_all), axis=0), jnp.where(same, share, 0.0),
        precision=lax.Precision.HIGHEST, preferred_element_type=jnp.float32,
    ).astype(jnp.bfloat16)

    pl.semaphore_wait(barrier, devices - 1)

    lower, upper = (place(lax.rem(me + devices - 1, devices)), place(lax.rem(me + 1, devices)))

    def edge_copy(phase, d, target):
        return pltpu.make_async_remote_copy(
            src_ref=snd.at[phase, d],
            dst_ref=rcv.at[phase, d],
            send_sem=snd_sem.at[phase, d],
            recv_sem=rcv_sem.at[phase, d],
            device_id=target,
            device_id_type=pl.DeviceIdType.MESH,
        )

    def edge_start(phase):
        down, up = edge_copy(phase, 0, lower), edge_copy(phase, 1, upper)

        @pl.when(me > 0)
        def _():
            down.start()

        @pl.when(me < devices - 1)
        def _():
            up.start()

    def edge_wait(phase):
        down, up = edge_copy(phase, 0, lower), edge_copy(phase, 1, upper)

        @pl.when(me > 0)
        def _():
            up.wait_recv()
            down.wait_send()

        @pl.when(me < devices - 1)
        def _():
            down.wait_recv()
            up.wait_send()

    edge_start(0)

    @pl.loop(0, slots // LANES, unroll=2)
    def _(tile):
        at = pl.multiple_of(tile * LANES, LANES)
        element = jnp.broadcast_to(felem[:, pl.ds(at, LANES)], (8, LANES))
        low = jnp.bitwise_and(element, LANES - 1)
        high = lax.shift_right_logical(element, 7)
        found = jnp.zeros((8, LANES), jnp.int32)
        for t in range(elems // LANES):
            got = jnp.take_along_axis(
                conn[:, t * LANES : (t + 1) * LANES], low, axis=1, mode="promise_in_bounds"
            )
            found = jnp.where(high == t, got, found)
        slot_node[:, pl.ds(at, LANES)] = found

    lane = lax.broadcasted_iota(jnp.int32, (8, LANES), 1)
    coarse_iota = lax.broadcasted_iota(jnp.int32, (CE_DEV, LANES), 0)
    group_tiles = GROUP * CAP // LANES

    @pl.loop(0, devices // GROUP)
    def _(group):
        base = group * (GROUP * CAP)
        ids = [
            jnp.broadcast_to(
                celem[:, pl.ds(pl.multiple_of(base + t * LANES, LANES), LANES)], (8, LANES)
            )
            for t in range(group_tiles)
        ]
        for o in range(GROUP):
            owner = spread([ids, ids, ids], lane, o)
            hit = coarse_iota == owner[0:1, :]
            at = pl.multiple_of((group * GROUP + o) * LANES, LANES)
            selector[:, pl.ds(at, LANES)] = jnp.where(hit, 1.0, 0.0).astype(jnp.bfloat16)

    def fill_edges():
        @pl.when(me > 0)
        def _():
            for a, field in enumerate((resid, scale)):
                for c in range(3):
                    at, to = (c * stride, (a * 3 + c) * edge)
                    field[at : at + edge, :] = get_edge(0, 1, to, edge)

        @pl.when(me < devices - 1)
        def _():
            for a, field in enumerate((resid, scale)):
                for c in range(3):
                    at, to = (c * stride + edge + owned, (a * 3 + c) * edge)
                    field[at : at + edge, :] = get_edge(0, 0, to, edge)

        direction[...] = scale[...] * resid[...] / THETA

    def add_edges(phase, add):
        def from_side(d, begin):
            for c in range(3):
                at = slice(c * stride + begin, c * stride + begin + window)
                theirs = get_edge(phase, d, c * window, window)
                resid[at, :] -= theirs
                direction[at, :] -= add * scale[at, :] * theirs

        def clear(begin):
            for c in range(3):
                at = c * stride + begin
                resid[at : at + edge, :] = jnp.zeros((edge, ROW), jnp.float32)

        @pl.when(me > 0)
        def _():
            from_side(1, 0)

        @pl.when(me == 0)
        def _():
            clear(0)

        @pl.when(me < devices - 1)
        def _():
            from_side(0, owned)

        @pl.when(me == devices - 1)
        def _():
            clear(edge + owned)

    tables = (table_a, table_b)
    for side in tables:
        side[...] = jnp.zeros_like(side)
    direction[...] = scale[...] * resid[...] / THETA
    total[...] = jnp.zeros_like(total)

    per_row = ROW // LANES
    inner = range(window * per_row, owned * per_row)
    outer = [h for h in range(rows * per_row) if h not in inner]

    def gather(field, index, hs, out):
        low = [jnp.bitwise_and(i, LANES - 1) for i in index]
        high = [lax.shift_right_logical(i, 7) for i in index]
        for h in hs:
            at, side = divmod(h, per_row)
            here = [i == h for i in high]
            for c in range(3):
                r = c * stride + at
                row = field[r : r + 1, side * LANES : (side + 1) * LANES]
                for t in range(len(index)):
                    out[c][t] = jnp.where(here[t], pick(row, low[t]), out[c][t])
        return out

    def gather_local(hs, first):
        @pl.loop(0, elems // (LANES * TILES))
        def _(chunk):
            starts = [pl.multiple_of((chunk * TILES + t) * LANES, LANES) for t in range(TILES)]
            index = [conn[:, pl.ds(s, LANES)] for s in starts]
            out = [
                [
                    jnp.zeros((8, LANES), jnp.float32)
                    if first
                    else local[c * 8 : (c + 1) * 8, pl.ds(starts[t], LANES)]
                    for t in range(TILES)
                ]
                for c in range(3)
            ]
            got = gather(direction, index, hs, out)
            for c in range(3):
                for t in range(TILES):
                    local[c * 8 : (c + 1) * 8, pl.ds(starts[t], LANES)] = got[c][t]

    steps = schedule()

    def outer_of(field, c):
        low, high = (slice(c * stride + at, c * stride + at + window) for at in (0, owned))
        return jnp.concatenate([field[low, :], field[high, :]], axis=0)

    def inner_of(field):
        return [field[c * stride + window : c * stride + owned, :] for c in range(3)]

    def scatter(rows_of, count):
        iota = lax.broadcasted_iota(jnp.int32, (count, elems), 0)
        height = 3 * TERMS * count
        empty = [jnp.zeros((-height % 32, elems), jnp.float32)] if height % 32 else []
        got = None
        for j in range(8):
            hit = iota == rows_of[j : j + 1, :]
            left = jnp.concatenate(
                [
                    jnp.where(hit, split_f[s * 24 + c * 8 + j : s * 24 + c * 8 + j + 1, :], 0.0)
                    for s in range(TERMS)
                    for c in range(3)
                ]
                + empty,
                axis=0,
            ).astype(F8)
            more = jnp.dot(left, onehot_t[j], preferred_element_type=jnp.float32)
            got = more if got is None else got + more
        return [
            joined([got[(s * 3 + c) * count : (s * 3 + c + 1) * count, :] for s in range(TERMS)])
            for c in range(3)
        ]

    @pl.loop(0, SWEEPS)
    def _(sweep):
        gather_local(inner, True)
        force_e[...] = jnp.dot(
            k_ref[...], local[...], precision=lax.Precision.HIGHEST,
            preferred_element_type=jnp.float32,
        )
        top_inner = functools.reduce(jnp.maximum, [largest(v) for v in inner_of(direction)])
        edge_wait(sweep)

        @pl.when(sweep == 0)
        def _():
            fill_edges()

        @pl.when(sweep > 0)
        def _():
            add_edges(sweep, jnp.where(sweep == 1, steps[0][1], steps[1][1]))

        ends = [outer_of(direction, c) for c in range(3)]
        top = largest(functools.reduce(jnp.maximum, [jnp.abs(v) for v in ends]))
        held = [terms(v * (TOP / jnp.maximum(top, TINY))) for v in ends]
        for t, side in enumerate(tables):
            lanes = slice(t * LANES, (t + 1) * LANES)
            for q in range(8):
                side[pl.ds(q, span, stride=8), :] = held[q % 3][q // 3][:, lanes]
            side[8 * span : 9 * span, :] = held[2][2][:, lanes]
        nodes8 = jnp.concatenate([side[...] for side in tables], axis=1).astype(F8)
        iota = lax.broadcasted_iota(jnp.int32, (span, elems), 0)
        for j in range(8):
            row = jnp.broadcast_to(outer_row[j : j + 1, :], (8, elems))
            found = jnp.dot(nodes8, onehot[j], preferred_element_type=jnp.float32)
            first = jnp.zeros((8, elems), jnp.float32)
            for h in range(span):
                first = jnp.where(row == h, found[h * 8 : (h + 1) * 8, :], first)
            last = jnp.where(row == iota, found[8 * span : 9 * span, :], 0.0)
            picked[j * BLOCK : (j + 1) * BLOCK, :] = jnp.concatenate([first, last], axis=0).astype(
                jnp.bfloat16
            )
        moved = jnp.dot(spread_k[...], picked[...], preferred_element_type=jnp.float32)
        moved = moved[:24, :] + moved[24:, :]
        bound = jnp.maximum(reach * jnp.maximum(top, top_inner), TINY)
        forces = (force_e[...] + moved * (top * (1.0 / TOP))) * coefs[...]
        for s, v in enumerate(terms(forces * (TOP / bound))):
            split_f[s * 24 : (s + 1) * 24, :] = v

        unit = bound * (1.0 / TOP)
        keep = jnp.where(sweep == 0, steps[0][0], steps[1][0])
        add = jnp.where(sweep == 0, steps[0][1], steps[1][1])
        given = [v * unit for v in scatter(outer_row, span)]
        for d in range(2):
            for c in range(3):
                put_edge(sweep + 1, d, c * window, given[c][d * window : (d + 1) * window, :])
        edge_start(sweep + 1)
        total[...] += direction[...]

        def update(at, value):
            new = resid[at, :] - value
            resid[at, :] = new
            direction[at, :] = keep * direction[at, :] + add * scale[at, :] * new

        for c in range(3):
            for d, begin in enumerate((0, owned)):
                update(
                    slice(c * stride + begin, c * stride + begin + window),
                    given[c][d * window : (d + 1) * window, :],
                )
        middle = owned - window
        given = scatter(inner_row, -(-middle // 8) * 8)
        for c in range(3):
            update(slice(c * stride + window, c * stride + owned), given[c][:middle, :] * unit)

    @pl.loop(0, slots // LANES, unroll=2)
    def _(tile):
        at = pl.multiple_of(tile * LANES, LANES)
        begun = [[jnp.zeros((8, LANES), jnp.float32)] for _ in range(3)]
        got = gather(resid, [slot_node[:, pl.ds(at, LANES)]], inner, begun)
        for c in range(3):
            contrib[c * 8 : (c + 1) * 8, pl.ds(at, LANES)] = got[c][0]

    edge_wait(SWEEPS)
    add_edges(SWEEPS, 0.0)

    @pl.loop(0, slots // LANES, unroll=2)
    def _(tile):
        at = pl.multiple_of(tile * LANES, LANES)
        begun = [[contrib[c * 8 : (c + 1) * 8, pl.ds(at, LANES)]] for c in range(3)]
        got = gather(resid, [slot_node[:, pl.ds(at, LANES)]], outer, begun)
        for c in range(3):
            values[c * 8 : (c + 1) * 8, :] = got[c][0]
        for c in range(3):
            acc = jnp.zeros((8, LANES), jnp.float32)
            for j in range(8):
                acc = acc + weights[:, j, pl.ds(at, LANES)] * values[c * 8 + j : c * 8 + j + 1, :]
            contrib[c * 8 : (c + 1) * 8, pl.ds(at, LANES)] = acc

    lane_slot = jnp.bitwise_and(lane, SPACE - 1)

    @pl.loop(0, devices // GROUP)
    def _(group):
        base = group * (GROUP * CAP)
        tiles = [
            [
                contrib[
                    c * 8 : (c + 1) * 8,
                    pl.ds(pl.multiple_of(base + t * LANES, LANES), LANES),
                ]
                for t in range(group_tiles)
            ]
            for c in range(3)
        ]
        for o in range(GROUP):
            owner = group * GROUP + o
            live = (lane_slot < counts[0, owner]) & (lane < 3 * SPACE)
            sent[owner] = jnp.where(live, spread(tiles, lane, o), 0.0)

    def slot_copy(target):
        return pltpu.make_async_remote_copy(
            src_ref=sent.at[target],
            dst_ref=arrived.at[me],
            send_sem=out_sem.at[target],
            recv_sem=in_sem.at[me],
            device_id=place(target),
            device_id_type=pl.DeviceIdType.MESH,
        )

    def slot_arrival(source):
        return pltpu.make_async_remote_copy(
            src_ref=sent.at[source],
            dst_ref=arrived.at[source],
            send_sem=out_sem.at[source],
            recv_sem=in_sem.at[source],
            device_id=place(source),
            device_id_type=pl.DeviceIdType.MESH,
        )

    @pl.loop(1, devices)
    def _(step):
        slot_copy(lax.rem(me + step, devices)).start()

    own = pltpu.make_async_copy(sent.at[me], arrived.at[me], own_sem)
    own.start()

    for c in range(3):
        for h in range(owned):
            at = c * stride + edge + h
            smoothed[c : c + 1, h * ROW : (h + 1) * ROW] = total[at : at + 1, :]

    own.wait()

    @pl.loop(1, devices)
    def _(step):
        slot_arrival(lax.rem(me + step, devices)).wait_recv()

    @pl.loop(0, devices)
    def _(source):
        got = arrived[source]
        pieces = [
            split(jnp.where((lane >= c * SPACE) & (lane < (c + 1) * SPACE), got, 0.0))
            for c in range(3)
        ]
        stacked[:, pl.ds(pl.multiple_of(source * LANES, LANES), LANES)] = jnp.concatenate(
            [pieces[c][s] for s in range(2) for c in range(3)], axis=0
        ).astype(jnp.bfloat16)

    sums = lax.dot_general(
        stacked[...], selector[...], (((1,), (1,)), ((), ())), preferred_element_type=jnp.float32
    )
    load[...] = sums[:24, :] + sums[24:, :]

    @pl.loop(1, devices)
    def _(step):
        slot_copy(lax.rem(me + step, devices)).wait_send()


def on_device(sizes, force, inv_diag, k_ref, coefs, conn, felem, weights, counts, celem):
    devices = sizes[0] * sizes[1]
    nodes = force.shape[1]
    elems = conn.shape[1]
    slots = felem.shape[0]
    rows = (nodes + 2 * BAND) // ROW
    stride = -(-rows // 8) * 8
    edge_rows = 6 * BAND // ROW
    field = pltpu.VMEM((3 * stride, ROW), jnp.float32)
    edges = pltpu.VMEM((SWEEPS + 1, 2, edge_rows * ROW // LANES, LANES), jnp.float32)
    vmem = pl.BlockSpec(memory_space=pltpu.VMEM)
    hbm = pl.BlockSpec(memory_space=pltpu.HBM)
    given = (force, inv_diag, k_ref, coefs, conn, felem, weights, counts, celem)
    taken = [pltpu.with_memory_space_constraint(v, pltpu.HBM) for v in given]
    return pl.pallas_call(
        functools.partial(kernel, sizes),
        out_shape=(
            pltpu.VMEM((3, nodes), jnp.float32),
            pltpu.VMEM((24, CE_DEV), jnp.float32),
        ),
        in_specs=[hbm] * 9,
        out_specs=(vmem, vmem),
        scratch_shapes=[
            pltpu.VMEM((3, nodes), jnp.float32),
            pltpu.VMEM((3, nodes), jnp.float32),
            pltpu.VMEM((24, 24), jnp.float32),
            pltpu.VMEM((1, elems), jnp.float32),
            pltpu.VMEM((8, elems), jnp.int32),
            pltpu.VMEM((1, slots), jnp.int32),
            pltpu.VMEM((8, 8, slots), jnp.float32),
            pltpu.VMEM((1, slots), jnp.int32),
            pltpu.SMEM((1, devices), jnp.int32),
            field,
            field,
            field,
            field,
            pltpu.VMEM((24, elems), jnp.float32),
            pltpu.VMEM((24, elems), jnp.float32),
            pltpu.VMEM((24 * TERMS, elems), jnp.float32),
            pltpu.VMEM((8, elems), jnp.int32),
            pltpu.VMEM((8, elems), jnp.int32),
            pltpu.VMEM((8, ROW, elems), F8),
            pltpu.VMEM((8, elems, ROW), F8),
            pltpu.VMEM((PAD, LANES), jnp.float32),
            pltpu.VMEM((PAD, LANES), jnp.float32),
            pltpu.VMEM((8 * BLOCK, elems), jnp.bfloat16),
            pltpu.VMEM((48, 8 * BLOCK), jnp.bfloat16),
            pltpu.VMEM((8, slots), jnp.int32),
            pltpu.VMEM((24, LANES), jnp.float32),
            pltpu.VMEM((24, slots), jnp.float32),
            pltpu.VMEM((devices, 8, LANES), jnp.float32),
            pltpu.VMEM((CE_DEV, devices * LANES), jnp.bfloat16),
            pltpu.VMEM((devices, 8, LANES), jnp.float32),
            pltpu.VMEM((48, devices * LANES), jnp.bfloat16),
            edges,
            edges,
            pltpu.SemaphoreType.DMA((SWEEPS + 1, 2)),
            pltpu.SemaphoreType.DMA((SWEEPS + 1, 2)),
            pltpu.SemaphoreType.DMA((devices,)),
            pltpu.SemaphoreType.DMA((devices,)),
            pltpu.SemaphoreType.DMA,
            pltpu.SemaphoreType.DMA((9,)),
        ],
        compiler_params=pltpu.CompilerParams(
            collective_id=0, has_side_effects=True, vmem_limit_bytes=40 * 1024 * 1024
        ),
    )(*taken)


def solution(mesh):
    both = ("fine", "coarse")
    placed = (
        P(None, both),
        P(None, both),
        P(),
        P(both),
        P(None, both),
        P(both),
        P(None, None, both),
        P(both, None),
        P(both, None),
    )
    sizes = (mesh.shape["fine"], mesh.shape["coarse"])
    return jax.shard_map(
        functools.partial(on_device, sizes),
        mesh=mesh,
        in_specs=placed,
        out_specs=(P(None, both), P(None, both)),
        check_vma=False,
    )
```

```python
import functools

import jax
import jax.numpy as jnp
from jax import lax
from jax.experimental import pallas as pl
from jax.experimental.pallas import tpu as pltpu
from jax.sharding import PartitionSpec as P

BAND = 512
CAP = 24
CE_DEV = 128
LOW_END = 0.3
HIGH_END = 2.5
SWEEPS = 3
LANES = 128
ROW = 256
SPACE = 24
PARTS = 5
USED = 5
TERMS = 3
STEP = 16.0
TOP = 256.0
TINY = 1e-36
BLOCK = 16
PAD = 96
F8 = jnp.float8_e4m3fn
GROUP = 16
TILES = 2

THETA = (HIGH_END + LOW_END) / 2.0
DELTA = (HIGH_END - LOW_END) / 2.0
SIGMA = THETA / DELTA


def schedule():
    rho = 1.0 / SIGMA
    steps = []
    for _ in range(SWEEPS - 1):
        rho_new = 1.0 / (2.0 * SIGMA - rho)
        steps.append((rho_new * rho, 2.0 * rho_new / DELTA))
        rho = rho_new
    return steps + [(0.0, 0.0)]


def split(value):
    high = value.astype(jnp.bfloat16).astype(jnp.float32)
    return (high, value - high)


def terms(value):
    out = []
    for _ in range(TERMS):
        part = value.astype(F8).astype(jnp.float32)
        out.append(part)
        value = (value - part) * STEP
    return out


def largest(value):
    return jnp.max(jnp.abs(value), axis=(0, 1), keepdims=True)


def joined(parts):
    out = parts[-1]
    for part in parts[-2::-1]:
        out = part + out * (1.0 / STEP)
    return out


def pick(row, index):
    table = jnp.broadcast_to(row, index.shape)
    return jnp.take_along_axis(table, index, axis=1, mode="promise_in_bounds")


def spread(tiles, lane, local):
    first, at = divmod(local * CAP, LANES)
    out = None
    for c, row in enumerate(tiles):
        piece = pltpu.roll(row[first], (c * SPACE - at) % LANES, axis=1)
        left = LANES - at
        if left < CAP:
            rest = pltpu.roll(row[first + 1], (c * SPACE + left) % LANES, axis=1)
            piece = jnp.where(lane < c * SPACE + left, piece, rest)
        out = piece if c == 0 else jnp.where(lane < c * SPACE, out, piece)
    return out


def kernel(
    sizes, force_in, inv_diag_in, k_ref_in, coefs_in, conn_in, felem_in, weights_in, counts_in,
    celem_in, smoothed, load,
    force, inv_diag, k_ref, coefs, conn, felem, weights, celem, counts,
    direction, resid, scale, total, local, force_e, split_f, outer_row, inner_row, onehot,
    onehot_t, table_a, table_b, picked, spread_k, slot_node, values, contrib,
    sent, selector, arrived, stacked, snd, rcv,
    snd_sem, rcv_sem, out_sem, in_sem, load_sem,
):
    fine, coarse = sizes
    devices = fine * coarse
    me = lax.axis_index("fine") * coarse + lax.axis_index("coarse")
    nodes = force.shape[1]
    owned = nodes // ROW
    edge = BAND // ROW
    rows = owned + 2 * edge
    stride = total.shape[0] // 3
    elems = conn.shape[1]
    slots = felem.shape[1]
    window = 2 * edge

    half = snd.shape[2] // 2

    def put_edge(phase, d, to, value):
        count = value.shape[0]
        snd[phase, d, to : to + count, :] = value[:, :LANES]
        snd[phase, d, half + to : half + to + count, :] = value[:, LANES:]

    def get_edge(phase, d, to, count):
        return jnp.concatenate(
            [rcv[phase, d, at : at + count, :] for at in (to, half + to)], axis=1
        )

    def place(index):
        return (index // coarse, lax.rem(index, coarse))

    pairs = [
        (force_in, force), (inv_diag_in, inv_diag), (conn_in, conn), (felem_in, felem.at[0]),
        (celem_in, celem), (k_ref_in, k_ref), (coefs_in, coefs.at[0]), (weights_in, weights),
        (counts_in, counts),
    ]
    loads = [pltpu.make_async_copy(a, b, load_sem.at[n]) for n, (a, b) in enumerate(pairs)]
    for copy in loads:
        copy.start()

    barrier = pltpu.get_barrier_semaphore()

    @pl.loop(1, devices)
    def _(step):
        pl.semaphore_signal(
            barrier, inc=1, device_id=place(lax.rem(me + step, devices)),
            device_id_type=pl.DeviceIdType.MESH,
        )

    resid[...] = jnp.zeros_like(resid)
    scale[...] = jnp.zeros_like(scale)
    loads[0].wait()
    loads[1].wait()
    for c in range(3):
        for h in range(owned):
            at = c * stride + edge + h
            resid[at : at + 1, :] = force[c : c + 1, h * ROW : (h + 1) * ROW]
            scale[at : at + 1, :] = inv_diag[c : c + 1, h * ROW : (h + 1) * ROW]
    for d, begin in enumerate((edge, owned)):
        for a, field in enumerate((resid, scale)):
            for c in range(3):
                at = c * stride + begin
                to = (a * 3 + c) * edge
                put_edge(0, d, to, field[at : at + edge, :])

    for copy in loads[2:5]:
        copy.wait()

    span = window * 2
    node_row = lax.shift_right_logical(conn[...], 8)
    outer_row[...] = jnp.where(
        node_row < window, node_row, jnp.where(node_row < owned, span, node_row - owned + window)
    )
    inner_row[...] = node_row - window

    def as_bf16(index):
        return index.astype(jnp.float32).astype(jnp.bfloat16)

    one, none = jnp.bfloat16(1.0), jnp.bfloat16(0.0)

    @pl.loop(0, 8)
    def _(j):
        low = as_bf16(jnp.bitwise_and(conn[pl.ds(j, 1), :], ROW - 1))
        hit = as_bf16(lax.broadcasted_iota(jnp.int32, (ROW, elems), 0)) == low
        onehot[j] = jnp.where(hit, one, none).astype(F8)

    for t in range(elems // LANES):
        turned = jnp.transpose(
            jnp.bitwise_and(conn[:, t * LANES : (t + 1) * LANES], ROW - 1).astype(jnp.float32)
        )
        along = as_bf16(lax.broadcasted_iota(jnp.int32, (LANES, ROW), 1))
        for j in range(8):
            low = jnp.broadcast_to(turned[:, j : j + 1], (LANES, ROW)).astype(jnp.bfloat16)
            onehot_t[j, t * LANES : (t + 1) * LANES, :] = jnp.where(along == low, one, none).astype(F8)

    for copy in loads[5:]:
        copy.wait()

    k_all = k_ref[...]
    reach = largest(jnp.sum(jnp.abs(k_all), axis=1, keepdims=True)) * largest(coefs[...])
    column = lax.broadcasted_iota(jnp.int32, (24, 8 * BLOCK), 1)
    which_q = jnp.minimum(jnp.bitwise_and(column, BLOCK - 1), 3 * TERMS - 1)
    which_s = lax.shift_right_logical(which_q * 11, 5)
    dof = (which_q - which_s * 3) * 8 + lax.shift_right_logical(column, 4)
    same = lax.broadcasted_iota(jnp.int32, (24, 8 * BLOCK), 0) == dof
    share = jnp.where(which_s == 0, 1.0, jnp.where(which_s == 1, 1.0 / STEP, 1.0 / STEP**2))
    spread_k[...] = jnp.dot(
        jnp.concatenate(split(k_all), axis=0), jnp.where(same, share, 0.0),
        precision=lax.Precision.HIGHEST, preferred_element_type=jnp.float32,
    ).astype(jnp.bfloat16)

    pl.semaphore_wait(barrier, devices - 1)

    lower, upper = (place(lax.rem(me + devices - 1, devices)), place(lax.rem(me + 1, devices)))

    def edge_copy(phase, d, target):
        return pltpu.make_async_remote_copy(
            src_ref=snd.at[phase, d],
            dst_ref=rcv.at[phase, d],
            send_sem=snd_sem.at[phase, d],
            recv_sem=rcv_sem.at[phase, d],
            device_id=target,
            device_id_type=pl.DeviceIdType.MESH,
        )

    def edge_start(phase):
        down, up = edge_copy(phase, 0, lower), edge_copy(phase, 1, upper)

        @pl.when(me > 0)
        def _():
            down.start()

        @pl.when(me < devices - 1)
        def _():
            up.start()

    def edge_wait(phase):
        down, up = edge_copy(phase, 0, lower), edge_copy(phase, 1, upper)

        @pl.when(me > 0)
        def _():
            up.wait_recv()
            down.wait_send()

        @pl.when(me < devices - 1)
        def _():
            down.wait_recv()
            up.wait_send()

    edge_start(0)

    @pl.loop(0, slots // LANES, unroll=2)
    def _(tile):
        at = pl.multiple_of(tile * LANES, LANES)
        element = jnp.broadcast_to(felem[:, pl.ds(at, LANES)], (8, LANES))
        low = jnp.bitwise_and(element, LANES - 1)
        high = lax.shift_right_logical(element, 7)
        found = jnp.zeros((8, LANES), jnp.int32)
        for t in range(elems // LANES):
            got = jnp.take_along_axis(
                conn[:, t * LANES : (t + 1) * LANES], low, axis=1, mode="promise_in_bounds"
            )
            found = jnp.where(high == t, got, found)
        slot_node[:, pl.ds(at, LANES)] = found

    lane = lax.broadcasted_iota(jnp.int32, (8, LANES), 1)
    coarse_iota = as_bf16(lax.broadcasted_iota(jnp.int32, (LANES, CE_DEV), 1))
    sub = lax.broadcasted_iota(jnp.int32, (8, LANES), 0)
    group_tiles = GROUP * CAP // LANES

    @pl.loop(0, devices // GROUP)
    def _(group):
        base = group * (GROUP * CAP)
        ids = [
            jnp.broadcast_to(
                celem[:, pl.ds(pl.multiple_of(base + t * LANES, LANES), LANES)], (8, LANES)
            )
            for t in range(group_tiles)
        ]
        for first in range(0, GROUP, 8):
            rows8 = spread([ids] * PARTS, lane, first)
            for o in range(1, 8):
                rows8 = jnp.where(sub == o, spread([ids] * PARTS, lane, first + o), rows8)
            turned = jnp.transpose(rows8.astype(jnp.float32))
            for o in range(8):
                source = group * GROUP + first + o
                owner = jnp.broadcast_to(turned[:, o : o + 1], (LANES, CE_DEV))
                hit = coarse_iota == owner.astype(jnp.bfloat16)
                at = pl.multiple_of((source // coarse) * LANES, LANES)
                selector[lax.rem(source, coarse), pl.ds(at, LANES), :] = jnp.where(hit, one, none)

    def fill_edges():
        @pl.when(me > 0)
        def _():
            for a, field in enumerate((resid, scale)):
                for c in range(3):
                    at, to = (c * stride, (a * 3 + c) * edge)
                    field[at : at + edge, :] = get_edge(0, 1, to, edge)

        @pl.when(me < devices - 1)
        def _():
            for a, field in enumerate((resid, scale)):
                for c in range(3):
                    at, to = (c * stride + edge + owned, (a * 3 + c) * edge)
                    field[at : at + edge, :] = get_edge(0, 0, to, edge)

        direction[...] = scale[...] * resid[...] / THETA

    def add_edges(phase, add):
        def from_side(d, begin):
            for c in range(3):
                at = slice(c * stride + begin, c * stride + begin + window)
                theirs = get_edge(phase, d, c * window, window)
                resid[at, :] -= theirs
                direction[at, :] -= add * scale[at, :] * theirs

        def clear(begin):
            for c in range(3):
                at = c * stride + begin
                resid[at : at + edge, :] = jnp.zeros((edge, ROW), jnp.float32)

        @pl.when(me > 0)
        def _():
            from_side(1, 0)

        @pl.when(me == 0)
        def _():
            clear(0)

        @pl.when(me < devices - 1)
        def _():
            from_side(0, owned)

        @pl.when(me == devices - 1)
        def _():
            clear(edge + owned)

    tables = (table_a, table_b)
    for side in tables:
        side[...] = jnp.zeros_like(side)
    direction[...] = scale[...] * resid[...] / THETA
    total[...] = jnp.zeros_like(total)

    per_row = ROW // LANES
    inner = range(window * per_row, owned * per_row)
    outer = [h for h in range(rows * per_row) if h not in inner]

    def gather(field, index, hs, out):
        low = [jnp.bitwise_and(i, LANES - 1) for i in index]
        high = [lax.shift_right_logical(i, 7) for i in index]
        for h in hs:
            at, side = divmod(h, per_row)
            here = [i == h for i in high]
            for c in range(3):
                r = c * stride + at
                row = field[r : r + 1, side * LANES : (side + 1) * LANES]
                for t in range(len(index)):
                    out[c][t] = jnp.where(here[t], pick(row, low[t]), out[c][t])
        return out

    def gather_local(hs, first):
        @pl.loop(0, elems // (LANES * TILES))
        def _(chunk):
            starts = [pl.multiple_of((chunk * TILES + t) * LANES, LANES) for t in range(TILES)]
            index = [conn[:, pl.ds(s, LANES)] for s in starts]
            out = [
                [
                    jnp.zeros((8, LANES), jnp.float32)
                    if first
                    else local[c * 8 : (c + 1) * 8, pl.ds(starts[t], LANES)]
                    for t in range(TILES)
                ]
                for c in range(3)
            ]
            got = gather(direction, index, hs, out)
            for c in range(3):
                for t in range(TILES):
                    local[c * 8 : (c + 1) * 8, pl.ds(starts[t], LANES)] = got[c][t]

    steps = schedule()

    def outer_of(field, c):
        low, high = (slice(c * stride + at, c * stride + at + window) for at in (0, owned))
        return jnp.concatenate([field[low, :], field[high, :]], axis=0)

    def inner_of(field):
        return [field[c * stride + window : c * stride + owned, :] for c in range(3)]

    def scatter(rows_of, count):
        iota = lax.broadcasted_iota(jnp.int32, (count, elems), 0)
        height = 3 * TERMS * count
        empty = [jnp.zeros((-height % 32, elems), jnp.float32)] if height % 32 else []
        got = None
        for j in range(8):
            hit = iota == rows_of[j : j + 1, :]
            left = jnp.concatenate(
                [
                    jnp.where(hit, split_f[s * 24 + c * 8 + j : s * 24 + c * 8 + j + 1, :], 0.0)
                    for s in range(TERMS)
                    for c in range(3)
                ]
                + empty,
                axis=0,
            ).astype(F8)
            more = jnp.dot(left, onehot_t[j], preferred_element_type=jnp.float32)
            got = more if got is None else got + more
        return [
            joined([got[(s * 3 + c) * count : (s * 3 + c + 1) * count, :] for s in range(TERMS)])
            for c in range(3)
        ]

    @pl.loop(0, SWEEPS)
    def _(sweep):
        gather_local(inner, True)
        force_e[...] = jnp.dot(
            k_ref[...], local[...], precision=lax.Precision.HIGHEST,
            preferred_element_type=jnp.float32,
        )
        top_inner = functools.reduce(jnp.maximum, [largest(v) for v in inner_of(direction)])
        edge_wait(sweep)

        @pl.when(sweep == 0)
        def _():
            fill_edges()

        @pl.when(sweep > 0)
        def _():
            add_edges(sweep, jnp.where(sweep == 1, steps[0][1], steps[1][1]))

        ends = [outer_of(direction, c) for c in range(3)]
        top = largest(functools.reduce(jnp.maximum, [jnp.abs(v) for v in ends]))
        held = [terms(v * (TOP / jnp.maximum(top, TINY))) for v in ends]
        for t, side in enumerate(tables):
            lanes = slice(t * LANES, (t + 1) * LANES)
            for q in range(8):
                side[pl.ds(q, span, stride=8), :] = held[q % 3][q // 3][:, lanes]
            side[8 * span : 9 * span, :] = held[2][2][:, lanes]
        nodes8 = jnp.concatenate([side[...] for side in tables], axis=1).astype(F8)
        iota = lax.broadcasted_iota(jnp.int32, (span, elems), 0)
        for j in range(8):
            row = jnp.broadcast_to(outer_row[j : j + 1, :], (8, elems))
            found = jnp.dot(nodes8, onehot[j], preferred_element_type=jnp.float32)
            first = jnp.zeros((8, elems), jnp.float32)
            for h in range(span):
                first = jnp.where(row == h, found[h * 8 : (h + 1) * 8, :], first)
            last = jnp.where(row == iota, found[8 * span : 9 * span, :], 0.0)
            picked[j * BLOCK : (j + 1) * BLOCK, :] = jnp.concatenate([first, last], axis=0).astype(
                jnp.bfloat16
            )
        moved = jnp.dot(spread_k[...], picked[...], preferred_element_type=jnp.float32)
        moved = moved[:24, :] + moved[24:, :]
        bound = jnp.maximum(reach * jnp.maximum(top, top_inner), TINY)
        forces = (force_e[...] + moved * (top * (1.0 / TOP))) * coefs[...]
        for s, v in enumerate(terms(forces * (TOP / bound))):
            split_f[s * 24 : (s + 1) * 24, :] = v

        unit = bound * (1.0 / TOP)
        keep = jnp.where(sweep == 0, steps[0][0], steps[1][0])
        add = jnp.where(sweep == 0, steps[0][1], steps[1][1])
        given = [v * unit for v in scatter(outer_row, span)]
        for d in range(2):
            for c in range(3):
                put_edge(sweep + 1, d, c * window, given[c][d * window : (d + 1) * window, :])
        edge_start(sweep + 1)
        total[...] += direction[...]

        def update(at, value):
            new = resid[at, :] - value
            resid[at, :] = new
            direction[at, :] = keep * direction[at, :] + add * scale[at, :] * new

        for c in range(3):
            for d, begin in enumerate((0, owned)):
                update(
                    slice(c * stride + begin, c * stride + begin + window),
                    given[c][d * window : (d + 1) * window, :],
                )
        middle = owned - window
        given = scatter(inner_row, -(-middle // 8) * 8)
        for c in range(3):
            update(slice(c * stride + window, c * stride + owned), given[c][:middle, :] * unit)

    @pl.loop(0, slots // LANES, unroll=2)
    def _(tile):
        at = pl.multiple_of(tile * LANES, LANES)
        begun = [[jnp.zeros((8, LANES), jnp.float32)] for _ in range(3)]
        got = gather(resid, [slot_node[:, pl.ds(at, LANES)]], inner, begun)
        for c in range(3):
            contrib[c * 8 : (c + 1) * 8, pl.ds(at, LANES)] = got[c][0]

    edge_wait(SWEEPS)
    add_edges(SWEEPS, 0.0)

    def slot_copy(target):
        return pltpu.make_async_remote_copy(
            src_ref=sent.at[target, 0:USED],
            dst_ref=arrived.at[me, 0:USED],
            send_sem=out_sem.at[target],
            recv_sem=in_sem.at[me],
            device_id=place(target),
            device_id_type=pl.DeviceIdType.MESH,
        )

    def slot_arrival(source):
        return pltpu.make_async_remote_copy(
            src_ref=sent.at[source, 0:USED],
            dst_ref=arrived.at[source, 0:USED],
            send_sem=out_sem.at[source],
            recv_sem=in_sem.at[source],
            device_id=place(source),
            device_id_type=pl.DeviceIdType.MESH,
        )

    lane_part = lax.shift_right_logical(lane * 683, 14)
    lane_slot = lane - lane_part * SPACE
    groups = devices // GROUP

    @pl.loop(0, groups)
    def _(turn):
        group = turn
        base = group * (GROUP * CAP)
        tiles = [[] for _ in range(PARTS)]
        for t in range(group_tiles):
            at = pl.multiple_of(base + t * LANES, LANES)
            begun = [[contrib[c * 8 : (c + 1) * 8, pl.ds(at, LANES)]] for c in range(3)]
            got = gather(resid, [slot_node[:, pl.ds(at, LANES)]], outer, begun)
            accs = []
            for c in range(3):
                values[c * 8 : (c + 1) * 8, t * LANES : (t + 1) * LANES] = got[c][0]
                acc = jnp.zeros((8, LANES), jnp.float32)
                for j in range(8):
                    row = c * 8 + j
                    acc = acc + (
                        weights[:, j, pl.ds(at, LANES)]
                        * values[row : row + 1, t * LANES : (t + 1) * LANES]
                    )
                accs.append(acc)
            a, b, c = accs
            up = functools.partial(pltpu.roll, axis=0)
            for part, tile in enumerate(
                [
                    a, b, c, jnp.where(sub < 3, up(a, 3), up(b, 6)),
                    jnp.where(sub < 1, up(b, 1), up(c, 4)),
                ]
            ):
                tiles[part].append(tile)
        for o in range(GROUP):
            owner = group * GROUP + o
            live = (lane_slot < counts[0, owner]) & (lane < PARTS * SPACE)
            sent[owner] = jnp.where(live, spread(tiles, lane, o), 0.0)

        @pl.loop(0, GROUP)
        def _(step):
            target = group * GROUP + lax.rem(me + step, GROUP)

            @pl.when(target != me)
            def _():
                slot_copy(target).start()

    arrived[me] = sent[me]

    for c in range(3):
        for h in range(owned):
            at = c * stride + edge + h
            smoothed[c : c + 1, h * ROW : (h + 1) * ROW] = total[at : at + 1, :]

    sums = None
    for turn in range(coarse):
        side = lax.rem(me + turn, coarse)

        @pl.loop(0, fine)
        def _(f):
            source = f * coarse + side

            @pl.when(source != me)
            def _():
                slot_arrival(source).wait_recv()

            got = arrived[source]
            pieces = [
                split(jnp.where((lane_part == part) & (sub < USED), got, 0.0))
                for part in range(PARTS)
            ]
            stacked[:, pl.ds(pl.multiple_of(f * LANES, LANES), LANES)] = jnp.concatenate(
                [pieces[part][s] for s in range(2) for part in range(PARTS)], axis=0
            ).astype(jnp.bfloat16)

        more = jnp.dot(stacked[...], selector[side], preferred_element_type=jnp.float32)
        sums = more if sums is None else sums + more

    whole = sums[: PARTS * 8, :] + sums[PARTS * 8 :, :]
    for c in range(3):
        load[c * 8 : c * 8 + 5, :] = whole[c * 8 : c * 8 + 5, :]
    load[5:8, :] = whole[24:27, :]
    load[13:15, :] = whole[27:29, :]
    load[15:16, :] = whole[32:33, :]
    load[21:24, :] = whole[33:36, :]

    @pl.loop(1, devices)
    def _(step):
        slot_copy(lax.rem(me + step, devices)).wait_send()


def on_device(sizes, force, inv_diag, k_ref, coefs, conn, felem, weights, counts, celem):
    devices = sizes[0] * sizes[1]
    nodes = force.shape[1]
    elems = conn.shape[1]
    slots = felem.shape[0]
    rows = (nodes + 2 * BAND) // ROW
    stride = -(-rows // 8) * 8
    edge_rows = 6 * BAND // ROW
    field = pltpu.VMEM((3 * stride, ROW), jnp.float32)
    edges = pltpu.VMEM((SWEEPS + 1, 2, edge_rows * ROW // LANES, LANES), jnp.float32)
    vmem = pl.BlockSpec(memory_space=pltpu.VMEM)
    hbm = pl.BlockSpec(memory_space=pltpu.HBM)
    given = (force, inv_diag, k_ref, coefs, conn, felem, weights, counts, celem)
    taken = [pltpu.with_memory_space_constraint(v, pltpu.HBM) for v in given]
    return pl.pallas_call(
        functools.partial(kernel, sizes),
        out_shape=(
            pltpu.VMEM((3, nodes), jnp.float32),
            pltpu.VMEM((24, CE_DEV), jnp.float32),
        ),
        in_specs=[hbm] * 9,
        out_specs=(vmem, vmem),
        scratch_shapes=[
            pltpu.VMEM((3, nodes), jnp.float32),
            pltpu.VMEM((3, nodes), jnp.float32),
            pltpu.VMEM((24, 24), jnp.float32),
            pltpu.VMEM((1, elems), jnp.float32),
            pltpu.VMEM((8, elems), jnp.int32),
            pltpu.VMEM((1, slots), jnp.int32),
            pltpu.VMEM((8, 8, slots), jnp.float32),
            pltpu.VMEM((1, slots), jnp.int32),
            pltpu.SMEM((1, devices), jnp.int32),
            field,
            field,
            field,
            field,
            pltpu.VMEM((24, elems), jnp.float32),
            pltpu.VMEM((24, elems), jnp.float32),
            pltpu.VMEM((24 * TERMS, elems), jnp.float32),
            pltpu.VMEM((8, elems), jnp.int32),
            pltpu.VMEM((8, elems), jnp.int32),
            pltpu.VMEM((8, ROW, elems), F8),
            pltpu.VMEM((8, elems, ROW), F8),
            pltpu.VMEM((PAD, LANES), jnp.float32),
            pltpu.VMEM((PAD, LANES), jnp.float32),
            pltpu.VMEM((8 * BLOCK, elems), jnp.bfloat16),
            pltpu.VMEM((48, 8 * BLOCK), jnp.bfloat16),
            pltpu.VMEM((8, slots), jnp.int32),
            pltpu.VMEM((24, GROUP * CAP), jnp.float32),
            pltpu.VMEM((24, slots), jnp.float32),
            pltpu.VMEM((devices, 8, LANES), jnp.float32),
            pltpu.VMEM((sizes[1], sizes[0] * LANES, CE_DEV), jnp.bfloat16),
            pltpu.VMEM((devices, 8, LANES), jnp.float32),
            pltpu.VMEM((2 * PARTS * 8, sizes[0] * LANES), jnp.bfloat16),
            edges,
            edges,
            pltpu.SemaphoreType.DMA((SWEEPS + 1, 2)),
            pltpu.SemaphoreType.DMA((SWEEPS + 1, 2)),
            pltpu.SemaphoreType.DMA((devices,)),
            pltpu.SemaphoreType.DMA((devices,)),
            pltpu.SemaphoreType.DMA((9,)),
        ],
        compiler_params=pltpu.CompilerParams(
            collective_id=0, has_side_effects=True, vmem_limit_bytes=40 * 1024 * 1024
        ),
    )(*taken)


def solution(mesh):
    both = ("fine", "coarse")
    placed = (
        P(None, both),
        P(None, both),
        P(),
        P(both),
        P(None, both),
        P(both),
        P(None, None, both),
        P(both, None),
        P(both, None),
    )
    sizes = (mesh.shape["fine"], mesh.shape["coarse"])
    return jax.shard_map(
        functools.partial(on_device, sizes),
        mesh=mesh,
        in_specs=placed,
        out_specs=(P(None, both), P(None, both)),
        check_vma=False,
    )
```

```python
import functools

import jax
import jax.numpy as jnp
from jax import lax
from jax.experimental import pallas as pl
from jax.experimental.pallas import tpu as pltpu
from jax.sharding import PartitionSpec as P

BAND = 512
CAP = 24
CE_DEV = 128
LOW_END = 0.3
HIGH_END = 2.5
SWEEPS = 3
LANES = 128
ROW = 256
SPACE = 24
PARTS = 5
USED = 5
TERMS = 3
STEP = 16.0
TOP = 256.0
TINY = 1e-36
BLOCK = 16
PAD = 96
F8 = jnp.float8_e4m3fn
GROUP = 16
TILES = 2

THETA = (HIGH_END + LOW_END) / 2.0
DELTA = (HIGH_END - LOW_END) / 2.0
SIGMA = THETA / DELTA


def schedule():
    rho = 1.0 / SIGMA
    steps = []
    for _ in range(SWEEPS - 1):
        rho_new = 1.0 / (2.0 * SIGMA - rho)
        steps.append((rho_new * rho, 2.0 * rho_new / DELTA))
        rho = rho_new
    return steps + [(0.0, 0.0)]


def split(value):
    high = value.astype(jnp.bfloat16).astype(jnp.float32)
    return (high, value - high)


def terms(value):
    out = []
    for _ in range(TERMS):
        part = value.astype(F8).astype(jnp.float32)
        out.append(part)
        value = (value - part) * STEP
    return out


def largest(value):
    return jnp.max(jnp.abs(value), axis=(0, 1), keepdims=True)


def joined(parts):
    out = parts[-1]
    for part in parts[-2::-1]:
        out = part + out * (1.0 / STEP)
    return out


def pick(row, index):
    table = jnp.broadcast_to(row, index.shape)
    return jnp.take_along_axis(table, index, axis=1, mode="promise_in_bounds")


def spread(tiles, lane, local):
    first, at = divmod(local * CAP, LANES)
    out = None
    for c, row in enumerate(tiles):
        piece = pltpu.roll(row[first], (c * SPACE - at) % LANES, axis=1)
        left = LANES - at
        if left < CAP:
            rest = pltpu.roll(row[first + 1], (c * SPACE + left) % LANES, axis=1)
            piece = jnp.where(lane < c * SPACE + left, piece, rest)
        out = piece if c == 0 else jnp.where(lane < c * SPACE, out, piece)
    return out


def kernel(
    sizes, force_in, inv_diag_in, k_ref_in, coefs_in, conn_in, felem_in, weights_in, counts_in,
    celem_in, smoothed, load,
    force, inv_diag, k_ref, coefs, conn, felem, weights, celem, counts,
    direction, resid, scale, total, local, force_e, split_f, outer_row, inner_row, onehot,
    onehot_t, table_a, table_b, picked, spread_k, slot_node, values, contrib,
    sent, selector, arrived, stacked, snd, rcv,
    snd_sem, rcv_sem, out_sem, in_sem, load_sem,
):
    fine, coarse = sizes
    devices = fine * coarse
    me = lax.axis_index("fine") * coarse + lax.axis_index("coarse")
    nodes = force.shape[1]
    owned = nodes // ROW
    edge = BAND // ROW
    rows = owned + 2 * edge
    stride = total.shape[0] // 3
    elems = conn.shape[1]
    slots = felem.shape[1]
    window = 2 * edge

    half = snd.shape[2] // 2

    def put_edge(phase, d, to, value):
        count = value.shape[0]
        snd[phase, d, to : to + count, :] = value[:, :LANES]
        snd[phase, d, half + to : half + to + count, :] = value[:, LANES:]

    def get_edge(phase, d, to, count):
        return jnp.concatenate(
            [rcv[phase, d, at : at + count, :] for at in (to, half + to)], axis=1
        )

    def place(index):
        return (index // coarse, lax.rem(index, coarse))

    pairs = [
        (force_in, force), (inv_diag_in, inv_diag), (conn_in, conn), (felem_in, felem.at[0]),
        (celem_in, celem), (k_ref_in, k_ref), (coefs_in, coefs.at[0]), (weights_in, weights),
        (counts_in, counts),
    ]
    loads = [pltpu.make_async_copy(a, b, load_sem.at[n]) for n, (a, b) in enumerate(pairs)]
    for copy in loads:
        copy.start()

    barrier = pltpu.get_barrier_semaphore()

    @pl.loop(1, devices)
    def _(step):
        pl.semaphore_signal(
            barrier, inc=1, device_id=place(lax.rem(me + step, devices)),
            device_id_type=pl.DeviceIdType.MESH,
        )

    resid[...] = jnp.zeros_like(resid)
    scale[...] = jnp.zeros_like(scale)
    loads[0].wait()
    loads[1].wait()
    for c in range(3):
        for h in range(owned):
            at = c * stride + edge + h
            resid[at : at + 1, :] = force[c : c + 1, h * ROW : (h + 1) * ROW]
            scale[at : at + 1, :] = inv_diag[c : c + 1, h * ROW : (h + 1) * ROW]
    for d, begin in enumerate((edge, owned)):
        for a, field in enumerate((resid, scale)):
            for c in range(3):
                at = c * stride + begin
                to = (a * 3 + c) * edge
                put_edge(0, d, to, field[at : at + edge, :])

    for copy in loads[2:5]:
        copy.wait()

    span = window * 2
    node_row = lax.shift_right_logical(conn[...], 8)
    outer_row[...] = jnp.where(
        node_row < window, node_row, jnp.where(node_row < owned, span, node_row - owned + window)
    )
    inner_row[...] = node_row - window

    def as_bf16(index):
        return index.astype(jnp.float32).astype(jnp.bfloat16)

    one, none = jnp.bfloat16(1.0), jnp.bfloat16(0.0)

    @pl.loop(0, 8)
    def _(j):
        low = as_bf16(jnp.bitwise_and(conn[pl.ds(j, 1), :], ROW - 1))
        hit = as_bf16(lax.broadcasted_iota(jnp.int32, (ROW, elems), 0)) == low
        onehot[j] = jnp.where(hit, one, none).astype(F8)

    for t in range(elems // LANES):
        turned = jnp.transpose(
            jnp.bitwise_and(conn[:, t * LANES : (t + 1) * LANES], ROW - 1).astype(jnp.float32)
        )
        along = as_bf16(lax.broadcasted_iota(jnp.int32, (LANES, ROW), 1))
        for j in range(8):
            low = jnp.broadcast_to(turned[:, j : j + 1], (LANES, ROW)).astype(jnp.bfloat16)
            onehot_t[j, t * LANES : (t + 1) * LANES, :] = jnp.where(along == low, one, none).astype(F8)

    for copy in loads[5:]:
        copy.wait()

    k_all = k_ref[...]
    reach = largest(jnp.sum(jnp.abs(k_all), axis=1, keepdims=True)) * largest(coefs[...])
    column = lax.broadcasted_iota(jnp.int32, (24, 8 * BLOCK), 1)
    which_q = jnp.minimum(jnp.bitwise_and(column, BLOCK - 1), 3 * TERMS - 1)
    which_s = lax.shift_right_logical(which_q * 11, 5)
    dof = (which_q - which_s * 3) * 8 + lax.shift_right_logical(column, 4)
    same = lax.broadcasted_iota(jnp.int32, (24, 8 * BLOCK), 0) == dof
    share = jnp.where(which_s == 0, 1.0, jnp.where(which_s == 1, 1.0 / STEP, 1.0 / STEP**2))
    spread_k[...] = jnp.dot(
        jnp.concatenate(split(k_all), axis=0), jnp.where(same, share, 0.0),
        precision=lax.Precision.HIGHEST, preferred_element_type=jnp.float32,
    ).astype(jnp.bfloat16)

    pl.semaphore_wait(barrier, devices - 1)

    lower, upper = (place(lax.rem(me + devices - 1, devices)), place(lax.rem(me + 1, devices)))

    def edge_copy(phase, d, target):
        return pltpu.make_async_remote_copy(
            src_ref=snd.at[phase, d],
            dst_ref=rcv.at[phase, d],
            send_sem=snd_sem.at[phase, d],
            recv_sem=rcv_sem.at[phase, d],
            device_id=target,
            device_id_type=pl.DeviceIdType.MESH,
        )

    def edge_start(phase):
        down, up = edge_copy(phase, 0, lower), edge_copy(phase, 1, upper)

        @pl.when(me > 0)
        def _():
            down.start()

        @pl.when(me < devices - 1)
        def _():
            up.start()

    def edge_wait(phase):
        down, up = edge_copy(phase, 0, lower), edge_copy(phase, 1, upper)

        @pl.when(me > 0)
        def _():
            up.wait_recv()
            down.wait_send()

        @pl.when(me < devices - 1)
        def _():
            down.wait_recv()
            up.wait_send()

    edge_start(0)

    @pl.loop(0, slots // LANES, unroll=2)
    def _(tile):
        at = pl.multiple_of(tile * LANES, LANES)
        element = jnp.broadcast_to(felem[:, pl.ds(at, LANES)], (8, LANES))
        low = jnp.bitwise_and(element, LANES - 1)
        high = lax.shift_right_logical(element, 7)
        found = jnp.zeros((8, LANES), jnp.int32)
        for t in range(elems // LANES):
            got = jnp.take_along_axis(
                conn[:, t * LANES : (t + 1) * LANES], low, axis=1, mode="promise_in_bounds"
            )
            found = jnp.where(high == t, got, found)
        slot_node[:, pl.ds(at, LANES)] = found

    lane = lax.broadcasted_iota(jnp.int32, (8, LANES), 1)
    coarse_iota = as_bf16(lax.broadcasted_iota(jnp.int32, (LANES, CE_DEV), 1))
    sub = lax.broadcasted_iota(jnp.int32, (8, LANES), 0)
    group_tiles = GROUP * CAP // LANES

    @pl.loop(0, devices // GROUP)
    def _(group):
        base = group * (GROUP * CAP)
        ids = [
            jnp.broadcast_to(
                celem[:, pl.ds(pl.multiple_of(base + t * LANES, LANES), LANES)], (8, LANES)
            )
            for t in range(group_tiles)
        ]
        for first in range(0, GROUP, 8):
            rows8 = spread([ids] * PARTS, lane, first)
            for o in range(1, 8):
                rows8 = jnp.where(sub == o, spread([ids] * PARTS, lane, first + o), rows8)
            turned = jnp.transpose(rows8.astype(jnp.float32))
            for o in range(8):
                source = group * GROUP + first + o
                owner = jnp.broadcast_to(turned[:, o : o + 1], (LANES, CE_DEV))
                hit = coarse_iota == owner.astype(jnp.bfloat16)
                at = pl.multiple_of((source // coarse) * LANES, LANES)
                selector[lax.rem(source, coarse), pl.ds(at, LANES), :] = jnp.where(hit, one, none)

    def fill_edges():
        @pl.when(me > 0)
        def _():
            for a, field in enumerate((resid, scale)):
                for c in range(3):
                    at, to = (c * stride, (a * 3 + c) * edge)
                    field[at : at + edge, :] = get_edge(0, 1, to, edge)

        @pl.when(me < devices - 1)
        def _():
            for a, field in enumerate((resid, scale)):
                for c in range(3):
                    at, to = (c * stride + edge + owned, (a * 3 + c) * edge)
                    field[at : at + edge, :] = get_edge(0, 0, to, edge)

        direction[...] = scale[...] * resid[...] / THETA

    def add_edges(phase, add):
        def from_side(d, begin):
            for c in range(3):
                at = slice(c * stride + begin, c * stride + begin + window)
                theirs = get_edge(phase, d, c * window, window)
                resid[at, :] -= theirs
                direction[at, :] -= add * scale[at, :] * theirs

        def clear(begin):
            for c in range(3):
                at = c * stride + begin
                resid[at : at + edge, :] = jnp.zeros((edge, ROW), jnp.float32)

        @pl.when(me > 0)
        def _():
            from_side(1, 0)

        @pl.when(me == 0)
        def _():
            clear(0)

        @pl.when(me < devices - 1)
        def _():
            from_side(0, owned)

        @pl.when(me == devices - 1)
        def _():
            clear(edge + owned)

    tables = (table_a, table_b)
    for side in tables:
        side[...] = jnp.zeros_like(side)
    direction[...] = scale[...] * resid[...] / THETA
    total[...] = jnp.zeros_like(total)

    per_row = ROW // LANES
    inner = range(window * per_row, owned * per_row)
    outer = [h for h in range(rows * per_row) if h not in inner]

    def gather(field, index, hs, out):
        low = [jnp.bitwise_and(i, LANES - 1) for i in index]
        high = [lax.shift_right_logical(i, 7) for i in index]
        for h in hs:
            at, side = divmod(h, per_row)
            here = [i == h for i in high]
            for c in range(3):
                r = c * stride + at
                row = field[r : r + 1, side * LANES : (side + 1) * LANES]
                for t in range(len(index)):
                    out[c][t] = jnp.where(here[t], pick(row, low[t]), out[c][t])
        return out

    def gather_local(hs, first):
        @pl.loop(0, elems // (LANES * TILES))
        def _(chunk):
            starts = [pl.multiple_of((chunk * TILES + t) * LANES, LANES) for t in range(TILES)]
            index = [conn[:, pl.ds(s, LANES)] for s in starts]
            out = [
                [
                    jnp.zeros((8, LANES), jnp.float32)
                    if first
                    else local[c * 8 : (c + 1) * 8, pl.ds(starts[t], LANES)]
                    for t in range(TILES)
                ]
                for c in range(3)
            ]
            got = gather(direction, index, hs, out)
            for c in range(3):
                for t in range(TILES):
                    local[c * 8 : (c + 1) * 8, pl.ds(starts[t], LANES)] = got[c][t]

    steps = schedule()

    def outer_of(field, c):
        low, high = (slice(c * stride + at, c * stride + at + window) for at in (0, owned))
        return jnp.concatenate([field[low, :], field[high, :]], axis=0)

    def inner_of(field):
        return [field[c * stride + window : c * stride + owned, :] for c in range(3)]

    def scatter(rows_of, count):
        iota = lax.broadcasted_iota(jnp.int32, (count, elems), 0)
        height = 3 * TERMS * count
        empty = [jnp.zeros((-height % 32, elems), jnp.float32)] if height % 32 else []
        got = None
        for j in range(8):
            hit = iota == rows_of[j : j + 1, :]
            left = jnp.concatenate(
                [
                    jnp.where(hit, split_f[s * 24 + c * 8 + j : s * 24 + c * 8 + j + 1, :], 0.0)
                    for s in range(TERMS)
                    for c in range(3)
                ]
                + empty,
                axis=0,
            ).astype(F8)
            more = jnp.dot(left, onehot_t[j], preferred_element_type=jnp.float32)
            got = more if got is None else got + more
        return [
            joined([got[(s * 3 + c) * count : (s * 3 + c + 1) * count, :] for s in range(TERMS)])
            for c in range(3)
        ]

    @pl.loop(0, SWEEPS)
    def _(sweep):
        gather_local(inner, True)
        force_e[...] = jnp.dot(
            k_ref[...], local[...], precision=lax.Precision.HIGHEST,
            preferred_element_type=jnp.float32,
        )
        top_inner = functools.reduce(jnp.maximum, [largest(v) for v in inner_of(direction)])
        edge_wait(sweep)

        @pl.when(sweep == 0)
        def _():
            fill_edges()

        @pl.when(sweep > 0)
        def _():
            add_edges(sweep, jnp.where(sweep == 1, steps[0][1], steps[1][1]))

        ends = [outer_of(direction, c) for c in range(3)]
        top = largest(functools.reduce(jnp.maximum, [jnp.abs(v) for v in ends]))
        held = [terms(v * (TOP / jnp.maximum(top, TINY))) for v in ends]
        for t, side in enumerate(tables):
            lanes = slice(t * LANES, (t + 1) * LANES)
            for q in range(8):
                side[pl.ds(q, span, stride=8), :] = held[q % 3][q // 3][:, lanes]
            side[8 * span : 9 * span, :] = held[2][2][:, lanes]
        nodes8 = jnp.concatenate([side[...] for side in tables], axis=1).astype(F8)
        iota = lax.broadcasted_iota(jnp.int32, (span, elems), 0)
        for j in range(8):
            row = jnp.broadcast_to(outer_row[j : j + 1, :], (8, elems))
            found = jnp.dot(nodes8, onehot[j], preferred_element_type=jnp.float32)
            first = jnp.zeros((8, elems), jnp.float32)
            for h in range(span):
                first = jnp.where(row == h, found[h * 8 : (h + 1) * 8, :], first)
            last = jnp.where(row == iota, found[8 * span : 9 * span, :], 0.0)
            picked[j * BLOCK : (j + 1) * BLOCK, :] = jnp.concatenate([first, last], axis=0).astype(
                jnp.bfloat16
            )
        moved = jnp.dot(spread_k[...], picked[...], preferred_element_type=jnp.float32)
        moved = moved[:24, :] + moved[24:, :]
        bound = jnp.maximum(reach * jnp.maximum(top, top_inner), TINY)
        forces = (force_e[...] + moved * (top * (1.0 / TOP))) * coefs[...]
        for s, v in enumerate(terms(forces * (TOP / bound))):
            split_f[s * 24 : (s + 1) * 24, :] = v

        unit = bound * (1.0 / TOP)
        keep = jnp.where(sweep == 0, steps[0][0], steps[1][0])
        add = jnp.where(sweep == 0, steps[0][1], steps[1][1])
        given = [v * unit for v in scatter(outer_row, span)]
        for d in range(2):
            for c in range(3):
                put_edge(sweep + 1, d, c * window, given[c][d * window : (d + 1) * window, :])
        edge_start(sweep + 1)
        total[...] += direction[...]

        def update(at, value):
            new = resid[at, :] - value
            resid[at, :] = new
            direction[at, :] = keep * direction[at, :] + add * scale[at, :] * new

        for c in range(3):
            for d, begin in enumerate((0, owned)):
                update(
                    slice(c * stride + begin, c * stride + begin + window),
                    given[c][d * window : (d + 1) * window, :],
                )
        middle = owned - window
        given = scatter(inner_row, -(-middle // 8) * 8)
        for c in range(3):
            update(slice(c * stride + window, c * stride + owned), given[c][:middle, :] * unit)

    @pl.loop(0, slots // LANES, unroll=2)
    def _(tile):
        at = pl.multiple_of(tile * LANES, LANES)
        begun = [[jnp.zeros((8, LANES), jnp.float32)] for _ in range(3)]
        got = gather(resid, [slot_node[:, pl.ds(at, LANES)]], inner, begun)
        for c in range(3):
            contrib[c * 8 : (c + 1) * 8, pl.ds(at, LANES)] = got[c][0]

    edge_wait(SWEEPS)
    add_edges(SWEEPS, 0.0)

    def slot_copy(target):
        return pltpu.make_async_remote_copy(
            src_ref=sent.at[target, 0:USED],
            dst_ref=arrived.at[me, 0:USED],
            send_sem=out_sem.at[target],
            recv_sem=in_sem.at[me],
            device_id=place(target),
            device_id_type=pl.DeviceIdType.MESH,
        )

    def slot_arrival(source):
        return pltpu.make_async_remote_copy(
            src_ref=sent.at[source, 0:USED],
            dst_ref=arrived.at[source, 0:USED],
            send_sem=out_sem.at[source],
            recv_sem=in_sem.at[source],
            device_id=place(source),
            device_id_type=pl.DeviceIdType.MESH,
        )

    lane_part = lax.shift_right_logical(lane * 683, 14)
    lane_slot = lane - lane_part * SPACE
    groups = devices // GROUP

    @pl.loop(0, groups)
    def _(turn):
        group = turn
        base = group * (GROUP * CAP)
        tiles = [[] for _ in range(PARTS)]
        for t in range(group_tiles):
            at = pl.multiple_of(base + t * LANES, LANES)
            begun = [[contrib[c * 8 : (c + 1) * 8, pl.ds(at, LANES)]] for c in range(3)]
            got = gather(resid, [slot_node[:, pl.ds(at, LANES)]], outer, begun)
            accs = []
            for c in range(3):
                values[c * 8 : (c + 1) * 8, t * LANES : (t + 1) * LANES] = got[c][0]
                acc = jnp.zeros((8, LANES), jnp.float32)
                for j in range(8):
                    row = c * 8 + j
                    acc = acc + (
                        weights[:, j, pl.ds(at, LANES)]
                        * values[row : row + 1, t * LANES : (t + 1) * LANES]
                    )
                accs.append(acc)
            a, b, c = accs
            up = functools.partial(pltpu.roll, axis=0)
            for part, tile in enumerate(
                [
                    a, b, c, jnp.where(sub < 3, up(a, 3), up(b, 6)),
                    jnp.where(sub < 1, up(b, 1), up(c, 4)),
                ]
            ):
                tiles[part].append(tile)
        for o in range(GROUP):
            owner = group * GROUP + o
            live = (lane_slot < counts[0, owner]) & (lane < PARTS * SPACE)
            sent[owner] = jnp.where(live, spread(tiles, lane, o), 0.0)

        @pl.loop(0, GROUP)
        def _(step):
            target = group * GROUP + lax.rem(me + step, GROUP)

            @pl.when(target != me)
            def _():
                slot_copy(target).start()

    arrived[me] = sent[me]

    for c in range(3):
        for h in range(owned):
            at = c * stride + edge + h
            smoothed[c : c + 1, h * ROW : (h + 1) * ROW] = total[at : at + 1, :]

    sums = None
    for turn in range(coarse):
        side = lax.rem(me + turn, coarse)

        @pl.loop(0, fine)
        def _(f):
            source = f * coarse + side

            @pl.when(source != me)
            def _():
                slot_arrival(source).wait_recv()

            got = arrived[source]
            pieces = [
                split(jnp.where((lane_part == part) & (sub < USED), got, 0.0))
                for part in range(PARTS)
            ]
            stacked[:, pl.ds(pl.multiple_of(f * LANES, LANES), LANES)] = jnp.concatenate(
                [pieces[part][s] for s in range(2) for part in range(PARTS)], axis=0
            ).astype(jnp.bfloat16)

        more = jnp.dot(stacked[...], selector[side], preferred_element_type=jnp.float32)
        sums = more if sums is None else sums + more

    whole = sums[: PARTS * 8, :] + sums[PARTS * 8 :, :]
    for c in range(3):
        load[c * 8 : c * 8 + 5, :] = whole[c * 8 : c * 8 + 5, :]
    load[5:8, :] = whole[24:27, :]
    load[13:15, :] = whole[27:29, :]
    load[15:16, :] = whole[32:33, :]
    load[21:24, :] = whole[33:36, :]

    @pl.loop(1, devices)
    def _(step):
        slot_copy(lax.rem(me + step, devices)).wait_send()


def hand_over(smoothed, load, smoothed_out, load_out, sem):
    pairs = ((smoothed, smoothed_out), (load, load_out))
    copies = [pltpu.make_async_copy(a, b, sem.at[n]) for n, (a, b) in enumerate(pairs)]
    for copy in copies:
        copy.start()
    for copy in copies:
        copy.wait()


def on_device(sizes, force, inv_diag, k_ref, coefs, conn, felem, weights, counts, celem):
    devices = sizes[0] * sizes[1]
    nodes = force.shape[1]
    elems = conn.shape[1]
    slots = felem.shape[0]
    rows = (nodes + 2 * BAND) // ROW
    stride = -(-rows // 8) * 8
    edge_rows = 6 * BAND // ROW
    field = pltpu.VMEM((3 * stride, ROW), jnp.float32)
    edges = pltpu.VMEM((SWEEPS + 1, 2, edge_rows * ROW // LANES, LANES), jnp.float32)
    vmem = pl.BlockSpec(memory_space=pltpu.VMEM)
    hbm = pl.BlockSpec(memory_space=pltpu.HBM)
    given = (force, inv_diag, k_ref, coefs, conn, felem, weights, counts, celem)
    taken = [pltpu.with_memory_space_constraint(v, pltpu.HBM) for v in given]
    outs = pl.pallas_call(
        functools.partial(kernel, sizes),
        out_shape=(
            pltpu.VMEM((3, nodes), jnp.float32),
            pltpu.VMEM((24, CE_DEV), jnp.float32),
        ),
        in_specs=[hbm] * 9,
        out_specs=(vmem, vmem),
        scratch_shapes=[
            pltpu.VMEM((3, nodes), jnp.float32),
            pltpu.VMEM((3, nodes), jnp.float32),
            pltpu.VMEM((24, 24), jnp.float32),
            pltpu.VMEM((1, elems), jnp.float32),
            pltpu.VMEM((8, elems), jnp.int32),
            pltpu.VMEM((1, slots), jnp.int32),
            pltpu.VMEM((8, 8, slots), jnp.float32),
            pltpu.VMEM((1, slots), jnp.int32),
            pltpu.SMEM((1, devices), jnp.int32),
            field,
            field,
            field,
            field,
            pltpu.VMEM((24, elems), jnp.float32),
            pltpu.VMEM((24, elems), jnp.float32),
            pltpu.VMEM((24 * TERMS, elems), jnp.float32),
            pltpu.VMEM((8, elems), jnp.int32),
            pltpu.VMEM((8, elems), jnp.int32),
            pltpu.VMEM((8, ROW, elems), F8),
            pltpu.VMEM((8, elems, ROW), F8),
            pltpu.VMEM((PAD, LANES), jnp.float32),
            pltpu.VMEM((PAD, LANES), jnp.float32),
            pltpu.VMEM((8 * BLOCK, elems), jnp.bfloat16),
            pltpu.VMEM((48, 8 * BLOCK), jnp.bfloat16),
            pltpu.VMEM((8, slots), jnp.int32),
            pltpu.VMEM((24, GROUP * CAP), jnp.float32),
            pltpu.VMEM((24, slots), jnp.float32),
            pltpu.VMEM((devices, 8, LANES), jnp.float32),
            pltpu.VMEM((sizes[1], sizes[0] * LANES, CE_DEV), jnp.bfloat16),
            pltpu.VMEM((devices, 8, LANES), jnp.float32),
            pltpu.VMEM((2 * PARTS * 8, sizes[0] * LANES), jnp.bfloat16),
            edges,
            edges,
            pltpu.SemaphoreType.DMA((SWEEPS + 1, 2)),
            pltpu.SemaphoreType.DMA((SWEEPS + 1, 2)),
            pltpu.SemaphoreType.DMA((devices,)),
            pltpu.SemaphoreType.DMA((devices,)),
            pltpu.SemaphoreType.DMA((9,)),
        ],
        compiler_params=pltpu.CompilerParams(
            collective_id=0, has_side_effects=True, vmem_limit_bytes=40 * 1024 * 1024
        ),
    )(*taken)
    outs = [pltpu.with_memory_space_constraint(v, pltpu.VMEM) for v in outs]
    return pl.pallas_call(
        hand_over,
        out_shape=(
            jax.ShapeDtypeStruct((3, nodes), jnp.float32),
            jax.ShapeDtypeStruct((24, CE_DEV), jnp.float32),
        ),
        in_specs=[vmem, vmem],
        out_specs=(hbm, hbm),
        scratch_shapes=[pltpu.SemaphoreType.DMA((2,))],
    )(*outs)


def solution(mesh):
    both = ("fine", "coarse")
    placed = (
        P(None, both),
        P(None, both),
        P(),
        P(both),
        P(None, both),
        P(both),
        P(None, None, both),
        P(both, None),
        P(both, None),
    )
    sizes = (mesh.shape["fine"], mesh.shape["coarse"])
    return jax.shard_map(
        functools.partial(on_device, sizes),
        mesh=mesh,
        in_specs=placed,
        out_specs=(P(None, both), P(None, both)),
        check_vma=False,
    )
```

```python
import functools

import jax
import jax.numpy as jnp
from jax import lax
from jax.experimental import pallas as pl
from jax.experimental.pallas import tpu as pltpu
from jax.sharding import PartitionSpec as P

BAND = 512
CAP = 24
CE_DEV = 128
LOW_END = 0.3
HIGH_END = 2.5
SWEEPS = 3
LANES = 128
ROW = 256
SPACE = 24
PARTS = 5
USED = 5
TERMS = 3
STEP = 16.0
TOP = 256.0
TINY = 1e-36
BLOCK = 16
PAD = 96
ASIDE = 4
F8 = jnp.float8_e4m3fn
GROUP = 16
TILES = 2

THETA = (HIGH_END + LOW_END) / 2.0
DELTA = (HIGH_END - LOW_END) / 2.0
SIGMA = THETA / DELTA


def schedule():
    rho = 1.0 / SIGMA
    steps = []
    for _ in range(SWEEPS - 1):
        rho_new = 1.0 / (2.0 * SIGMA - rho)
        steps.append((rho_new * rho, 2.0 * rho_new / DELTA))
        rho = rho_new
    return steps + [(0.0, 0.0)]


def split(value):
    high = value.astype(jnp.bfloat16).astype(jnp.float32)
    return (high, value - high)


def terms(value):
    out = []
    for _ in range(TERMS):
        part = value.astype(F8).astype(jnp.float32)
        out.append(part)
        value = (value - part) * STEP
    return out


def largest(value):
    return jnp.max(jnp.abs(value), axis=(0, 1), keepdims=True)


def joined(parts):
    out = parts[-1]
    for part in parts[-2::-1]:
        out = part + out * (1.0 / STEP)
    return out


def pick(row, index):
    table = jnp.broadcast_to(row, index.shape)
    return jnp.take_along_axis(table, index, axis=1, mode="promise_in_bounds")


def spread(tiles, lane, local):
    first, at = divmod(local * CAP, LANES)
    out = None
    for c, row in enumerate(tiles):
        piece = pltpu.roll(row[first], (c * SPACE - at) % LANES, axis=1)
        left = LANES - at
        if left < CAP:
            rest = pltpu.roll(row[first + 1], (c * SPACE + left) % LANES, axis=1)
            piece = jnp.where(lane < c * SPACE + left, piece, rest)
        out = piece if c == 0 else jnp.where(lane < c * SPACE, out, piece)
    return out


def kernel(
    sizes, force_in, inv_diag_in, k_ref_in, coefs_in, conn_in, felem_in, weights_in, counts_in,
    celem_in, smoothed, load,
    force, inv_diag, k_ref, coefs, conn, felem, weights, celem, counts,
    direction, resid, scale, total, local, force_e, split_f, outer_row, inner_row, onehot,
    onehot_t, table_a, table_b, picked, spread_k, slot_node, values, contrib,
    sent, selector, arrived, stacked, snd, rcv,
    snd_sem, rcv_sem, out_sem, in_sem, load_sem,
):
    fine, coarse = sizes
    devices = fine * coarse
    me = lax.axis_index("fine") * coarse + lax.axis_index("coarse")
    nodes = force.shape[1]
    owned = nodes // ROW
    edge = BAND // ROW
    rows = owned + 2 * edge
    stride = total.shape[0] // 3
    elems = conn.shape[1]
    slots = felem.shape[1]
    window = 2 * edge

    half = snd.shape[2] // 2

    def put_edge(phase, d, to, value):
        count = value.shape[0]
        snd[phase, d, to : to + count, :] = value[:, :LANES]
        snd[phase, d, half + to : half + to + count, :] = value[:, LANES:]

    def get_edge(phase, d, to, count):
        return jnp.concatenate(
            [rcv[phase, d, at : at + count, :] for at in (to, half + to)], axis=1
        )

    def place(index):
        return (index // coarse, lax.rem(index, coarse))

    pairs = [
        (force_in, force), (inv_diag_in, inv_diag), (conn_in, conn), (felem_in, felem.at[0]),
        (celem_in, celem), (k_ref_in, k_ref), (coefs_in, coefs.at[0]), (weights_in, weights),
        (counts_in, counts),
    ]
    loads = [pltpu.make_async_copy(a, b, load_sem.at[n]) for n, (a, b) in enumerate(pairs)]
    for copy in loads:
        copy.start()

    barrier = pltpu.get_barrier_semaphore()

    @pl.loop(1, devices)
    def _(step):
        pl.semaphore_signal(
            barrier, inc=1, device_id=place(lax.rem(me + step, devices)),
            device_id_type=pl.DeviceIdType.MESH,
        )

    resid[...] = jnp.zeros_like(resid)
    scale[...] = jnp.zeros_like(scale)
    loads[0].wait()
    loads[1].wait()
    for c in range(3):
        for h in range(owned):
            at = c * stride + edge + h
            resid[at : at + 1, :] = force[c : c + 1, h * ROW : (h + 1) * ROW]
            scale[at : at + 1, :] = inv_diag[c : c + 1, h * ROW : (h + 1) * ROW]
    for d, begin in enumerate((edge, owned)):
        for a, field in enumerate((resid, scale)):
            for c in range(3):
                at = c * stride + begin
                to = (a * 3 + c) * edge
                put_edge(0, d, to, field[at : at + edge, :])

    for copy in loads[2:5]:
        copy.wait()

    span = window * 2
    node_row = lax.shift_right_logical(conn[...], 8)
    outer_row[...] = jnp.where(
        node_row < window, node_row, jnp.where(node_row < owned, span, node_row - owned + window)
    )
    inner_row[...] = node_row - window

    def as_bf16(index):
        return index.astype(jnp.float32).astype(jnp.bfloat16)

    one, none = jnp.bfloat16(1.0), jnp.bfloat16(0.0)

    @pl.loop(0, 8)
    def _(j):
        low = as_bf16(jnp.bitwise_and(conn[pl.ds(j, 1), :], ROW - 1))
        hit = as_bf16(lax.broadcasted_iota(jnp.int32, (ROW, elems), 0)) == low
        onehot[j] = jnp.where(hit, one, none).astype(F8)

    for t in range(elems // LANES):
        turned = jnp.transpose(
            jnp.bitwise_and(conn[:, t * LANES : (t + 1) * LANES], ROW - 1).astype(jnp.float32)
        )
        along = as_bf16(lax.broadcasted_iota(jnp.int32, (LANES, ROW), 1))
        for j in range(8):
            low = jnp.broadcast_to(turned[:, j : j + 1], (LANES, ROW)).astype(jnp.bfloat16)
            onehot_t[j, t * LANES : (t + 1) * LANES, :] = jnp.where(along == low, one, none).astype(F8)

    for copy in loads[5:]:
        copy.wait()

    k_all = k_ref[...]
    reach = largest(jnp.sum(jnp.abs(k_all), axis=1, keepdims=True)) * largest(coefs[...])
    column = lax.broadcasted_iota(jnp.int32, (24, 8 * BLOCK), 1)
    which_q = jnp.minimum(jnp.bitwise_and(column, BLOCK - 1), 3 * TERMS - 1)
    which_s = lax.shift_right_logical(which_q * 11, 5)
    dof = (which_q - which_s * 3) * 8 + lax.shift_right_logical(column, 4)
    same = lax.broadcasted_iota(jnp.int32, (24, 8 * BLOCK), 0) == dof
    share = jnp.where(which_s == 0, 1.0, jnp.where(which_s == 1, 1.0 / STEP, 1.0 / STEP**2))
    spread_k[...] = jnp.dot(
        jnp.concatenate(split(k_all), axis=0), jnp.where(same, share, 0.0),
        precision=lax.Precision.HIGHEST, preferred_element_type=jnp.float32,
    ).astype(jnp.bfloat16)

    pl.semaphore_wait(barrier, devices - 1)

    lower, upper = (place(lax.rem(me + devices - 1, devices)), place(lax.rem(me + 1, devices)))

    def edge_copy(phase, d, target):
        return pltpu.make_async_remote_copy(
            src_ref=snd.at[phase, d],
            dst_ref=rcv.at[phase, d],
            send_sem=snd_sem.at[phase, d],
            recv_sem=rcv_sem.at[phase, d],
            device_id=target,
            device_id_type=pl.DeviceIdType.MESH,
        )

    def edge_start(phase):
        down, up = edge_copy(phase, 0, lower), edge_copy(phase, 1, upper)

        @pl.when(me > 0)
        def _():
            down.start()

        @pl.when(me < devices - 1)
        def _():
            up.start()

    def edge_wait(phase):
        down, up = edge_copy(phase, 0, lower), edge_copy(phase, 1, upper)

        @pl.when(me > 0)
        def _():
            up.wait_recv()
            down.wait_send()

        @pl.when(me < devices - 1)
        def _():
            down.wait_recv()
            up.wait_send()

    edge_start(0)

    @pl.loop(0, slots // LANES, unroll=2)
    def _(tile):
        at = pl.multiple_of(tile * LANES, LANES)
        element = jnp.broadcast_to(felem[:, pl.ds(at, LANES)], (8, LANES))
        low = jnp.bitwise_and(element, LANES - 1)
        high = lax.shift_right_logical(element, 7)
        found = jnp.zeros((8, LANES), jnp.int32)
        for t in range(elems // LANES):
            got = jnp.take_along_axis(
                conn[:, t * LANES : (t + 1) * LANES], low, axis=1, mode="promise_in_bounds"
            )
            found = jnp.where(high == t, got, found)
        slot_node[:, pl.ds(at, LANES)] = found

    lane = lax.broadcasted_iota(jnp.int32, (8, LANES), 1)
    coarse_iota = as_bf16(lax.broadcasted_iota(jnp.int32, (LANES, CE_DEV), 1))
    sub = lax.broadcasted_iota(jnp.int32, (8, LANES), 0)
    group_tiles = GROUP * CAP // LANES

    @pl.loop(0, devices // GROUP)
    def _(group):
        base = group * (GROUP * CAP)
        ids = [
            jnp.broadcast_to(
                celem[:, pl.ds(pl.multiple_of(base + t * LANES, LANES), LANES)], (8, LANES)
            )
            for t in range(group_tiles)
        ]
        for first in range(0, GROUP, 8):
            rows8 = spread([ids] * PARTS, lane, first)
            for o in range(1, 8):
                rows8 = jnp.where(sub == o, spread([ids] * PARTS, lane, first + o), rows8)
            turned = jnp.transpose(rows8.astype(jnp.float32))
            for o in range(8):
                source = group * GROUP + first + o
                owner = jnp.broadcast_to(turned[:, o : o + 1], (LANES, CE_DEV))
                hit = coarse_iota == owner.astype(jnp.bfloat16)
                at = pl.multiple_of((source // coarse) * LANES, LANES)
                selector[lax.rem(source, coarse), pl.ds(at, LANES), :] = jnp.where(hit, one, none)

    def fill_edges():
        @pl.when(me > 0)
        def _():
            for a, field in enumerate((resid, scale)):
                for c in range(3):
                    at, to = (c * stride, (a * 3 + c) * edge)
                    field[at : at + edge, :] = get_edge(0, 1, to, edge)

        @pl.when(me < devices - 1)
        def _():
            for a, field in enumerate((resid, scale)):
                for c in range(3):
                    at, to = (c * stride + edge + owned, (a * 3 + c) * edge)
                    field[at : at + edge, :] = get_edge(0, 0, to, edge)

        direction[...] = scale[...] * resid[...] / THETA

    def add_edges(phase, add):
        def from_side(d, begin):
            for c in range(3):
                at = slice(c * stride + begin, c * stride + begin + window)
                theirs = get_edge(phase, d, c * window, window)
                resid[at, :] -= theirs
                direction[at, :] -= add * scale[at, :] * theirs

        def clear(begin):
            for c in range(3):
                at = c * stride + begin
                resid[at : at + edge, :] = jnp.zeros((edge, ROW), jnp.float32)

        @pl.when(me > 0)
        def _():
            from_side(1, 0)

        @pl.when(me == 0)
        def _():
            clear(0)

        @pl.when(me < devices - 1)
        def _():
            from_side(0, owned)

        @pl.when(me == devices - 1)
        def _():
            clear(edge + owned)

    tables = (table_a, table_b)
    for side in tables:
        side[...] = jnp.zeros_like(side)
    direction[...] = scale[...] * resid[...] / THETA
    total[...] = jnp.zeros_like(total)

    per_row = ROW // LANES
    inner = range(window * per_row, owned * per_row)
    outer = [h for h in range(rows * per_row) if h not in inner]

    def gather(field, index, hs, out):
        low = [jnp.bitwise_and(i, LANES - 1) for i in index]
        high = [lax.shift_right_logical(i, 7) for i in index]
        for h in hs:
            at, side = divmod(h, per_row)
            here = [i == h for i in high]
            for c in range(3):
                r = c * stride + at
                row = field[r : r + 1, side * LANES : (side + 1) * LANES]
                for t in range(len(index)):
                    out[c][t] = jnp.where(here[t], pick(row, low[t]), out[c][t])
        return out

    def gather_local(hs, first):
        @pl.loop(0, elems // (LANES * TILES))
        def _(chunk):
            starts = [pl.multiple_of((chunk * TILES + t) * LANES, LANES) for t in range(TILES)]
            index = [conn[:, pl.ds(s, LANES)] for s in starts]
            out = [
                [
                    jnp.zeros((8, LANES), jnp.float32)
                    if first
                    else local[c * 8 : (c + 1) * 8, pl.ds(starts[t], LANES)]
                    for t in range(TILES)
                ]
                for c in range(3)
            ]
            got = gather(direction, index, hs, out)
            for c in range(3):
                for t in range(TILES):
                    local[c * 8 : (c + 1) * 8, pl.ds(starts[t], LANES)] = got[c][t]

    steps = schedule()

    def outer_of(field, c):
        low, high = (slice(c * stride + at, c * stride + at + window) for at in (0, owned))
        return jnp.concatenate([field[low, :], field[high, :]], axis=0)

    def inner_of(field):
        return [field[c * stride + window : c * stride + owned, :] for c in range(3)]

    def scatter(rows_of, count):
        iota = lax.broadcasted_iota(jnp.int32, (count, elems), 0)
        height = 3 * TERMS * count
        empty = [jnp.zeros((-height % 32, elems), jnp.float32)] if height % 32 else []
        got = None
        for j in range(8):
            hit = iota == rows_of[j : j + 1, :]
            left = jnp.concatenate(
                [
                    jnp.where(hit, split_f[s * 24 + c * 8 + j : s * 24 + c * 8 + j + 1, :], 0.0)
                    for s in range(TERMS)
                    for c in range(3)
                ]
                + empty,
                axis=0,
            ).astype(F8)
            more = jnp.dot(left, onehot_t[j], preferred_element_type=jnp.float32)
            got = more if got is None else got + more
        return [
            joined([got[(s * 3 + c) * count : (s * 3 + c + 1) * count, :] for s in range(TERMS)])
            for c in range(3)
        ]

    @pl.loop(0, SWEEPS)
    def _(sweep):
        gather_local(inner, True)
        force_e[...] = jnp.dot(
            k_ref[...], local[...], precision=lax.Precision.HIGHEST,
            preferred_element_type=jnp.float32,
        )
        top_inner = functools.reduce(jnp.maximum, [largest(v) for v in inner_of(direction)])
        edge_wait(sweep)

        @pl.when(sweep == 0)
        def _():
            fill_edges()

        @pl.when(sweep > 0)
        def _():
            add_edges(sweep, jnp.where(sweep == 1, steps[0][1], steps[1][1]))

        ends = [outer_of(direction, c) for c in range(3)]
        top = largest(functools.reduce(jnp.maximum, [jnp.abs(v) for v in ends]))
        held = [terms(v * (TOP / jnp.maximum(top, TINY))) for v in ends]
        for t, side in enumerate(tables):
            lanes = slice(t * LANES, (t + 1) * LANES)
            for q in range(8):
                side[pl.ds(q, span, stride=8), :] = held[q % 3][q // 3][:, lanes]
            side[8 * span : 9 * span, :] = held[2][2][:, lanes]
        nodes8 = jnp.concatenate([side[...] for side in tables], axis=1).astype(F8)
        wide = elems - ASIDE * LANES
        iota = lax.broadcasted_iota(jnp.int32, (span, wide), 0)
        aside = []
        for t in range(ASIDE):
            index = conn[:, wide + t * LANES : wide + (t + 1) * LANES]
            begun = [[jnp.zeros((8, LANES), jnp.float32)] for _ in range(3)]
            got = gather(direction, [index], outer, begun)
            aside.append(jnp.concatenate([got[c][0] for c in range(3)], axis=0))
        for j in range(8):
            row = jnp.broadcast_to(outer_row[j : j + 1, :wide], (8, wide))
            found = jnp.dot(nodes8, onehot[j, :, :wide], preferred_element_type=jnp.float32)
            first = jnp.zeros((8, wide), jnp.float32)
            for h in range(span):
                first = jnp.where(row == h, found[h * 8 : (h + 1) * 8, :], first)
            last = jnp.where(row == iota, found[8 * span : 9 * span, :], 0.0)
            picked[j * BLOCK : (j + 1) * BLOCK, :] = jnp.concatenate([first, last], axis=0).astype(
                jnp.bfloat16
            )
        moved = jnp.dot(spread_k[...], picked[...], preferred_element_type=jnp.float32)
        moved = (moved[:24, :] + moved[24:, :]) * (top * (1.0 / TOP))
        aside = jnp.dot(
            k_ref[...], jnp.concatenate(aside, axis=1), precision=lax.Precision.HIGHEST,
            preferred_element_type=jnp.float32,
        )
        moved = jnp.concatenate([moved, aside], axis=1)
        bound = jnp.maximum(reach * jnp.maximum(top, top_inner), TINY)
        forces = (force_e[...] + moved) * coefs[...]
        for s, v in enumerate(terms(forces * (TOP / bound))):
            split_f[s * 24 : (s + 1) * 24, :] = v

        unit = bound * (1.0 / TOP)
        keep = jnp.where(sweep == 0, steps[0][0], steps[1][0])
        add = jnp.where(sweep == 0, steps[0][1], steps[1][1])
        given = [v * unit for v in scatter(outer_row, span)]
        for d in range(2):
            for c in range(3):
                put_edge(sweep + 1, d, c * window, given[c][d * window : (d + 1) * window, :])
        edge_start(sweep + 1)
        total[...] += direction[...]

        def update(at, value):
            new = resid[at, :] - value
            resid[at, :] = new
            direction[at, :] = keep * direction[at, :] + add * scale[at, :] * new

        for c in range(3):
            for d, begin in enumerate((0, owned)):
                update(
                    slice(c * stride + begin, c * stride + begin + window),
                    given[c][d * window : (d + 1) * window, :],
                )
        middle = owned - window
        given = scatter(inner_row, -(-middle // 8) * 8)
        for c in range(3):
            update(slice(c * stride + window, c * stride + owned), given[c][:middle, :] * unit)

    @pl.loop(0, slots // LANES, unroll=2)
    def _(tile):
        at = pl.multiple_of(tile * LANES, LANES)
        begun = [[jnp.zeros((8, LANES), jnp.float32)] for _ in range(3)]
        got = gather(resid, [slot_node[:, pl.ds(at, LANES)]], inner, begun)
        for c in range(3):
            contrib[c * 8 : (c + 1) * 8, pl.ds(at, LANES)] = got[c][0]

    edge_wait(SWEEPS)
    add_edges(SWEEPS, 0.0)

    def slot_copy(target):
        return pltpu.make_async_remote_copy(
            src_ref=sent.at[target, 0:USED],
            dst_ref=arrived.at[me, 0:USED],
            send_sem=out_sem.at[target],
            recv_sem=in_sem.at[me],
            device_id=place(target),
            device_id_type=pl.DeviceIdType.MESH,
        )

    def slot_arrival(source):
        return pltpu.make_async_remote_copy(
            src_ref=sent.at[source, 0:USED],
            dst_ref=arrived.at[source, 0:USED],
            send_sem=out_sem.at[source],
            recv_sem=in_sem.at[source],
            device_id=place(source),
            device_id_type=pl.DeviceIdType.MESH,
        )

    lane_part = lax.shift_right_logical(lane * 683, 14)
    lane_slot = lane - lane_part * SPACE
    groups = devices // GROUP

    @pl.loop(0, groups)
    def _(turn):
        group = turn
        base = group * (GROUP * CAP)
        tiles = [[] for _ in range(PARTS)]
        for t in range(group_tiles):
            at = pl.multiple_of(base + t * LANES, LANES)
            begun = [[contrib[c * 8 : (c + 1) * 8, pl.ds(at, LANES)]] for c in range(3)]
            got = gather(resid, [slot_node[:, pl.ds(at, LANES)]], outer, begun)
            accs = []
            for c in range(3):
                values[c * 8 : (c + 1) * 8, t * LANES : (t + 1) * LANES] = got[c][0]
                acc = jnp.zeros((8, LANES), jnp.float32)
                for j in range(8):
                    row = c * 8 + j
                    acc = acc + (
                        weights[:, j, pl.ds(at, LANES)]
                        * values[row : row + 1, t * LANES : (t + 1) * LANES]
                    )
                accs.append(acc)
            a, b, c = accs
            up = functools.partial(pltpu.roll, axis=0)
            for part, tile in enumerate(
                [
                    a, b, c, jnp.where(sub < 3, up(a, 3), up(b, 6)),
                    jnp.where(sub < 1, up(b, 1), up(c, 4)),
                ]
            ):
                tiles[part].append(tile)
        for o in range(GROUP):
            owner = group * GROUP + o
            live = (lane_slot < counts[0, owner]) & (lane < PARTS * SPACE)
            sent[owner] = jnp.where(live, spread(tiles, lane, o), 0.0)

        @pl.loop(0, GROUP)
        def _(step):
            target = group * GROUP + lax.rem(me + step, GROUP)

            @pl.when(target != me)
            def _():
                slot_copy(target).start()

    arrived[me] = sent[me]

    for c in range(3):
        for h in range(owned):
            at = c * stride + edge + h
            smoothed[c : c + 1, h * ROW : (h + 1) * ROW] = total[at : at + 1, :]

    sums = None
    for turn in range(coarse):
        side = lax.rem(me + turn, coarse)

        if turn == coarse - 1:
            @pl.loop(1, devices)
            def _(step):
                slot_copy(lax.rem(me + step, devices)).wait_send()

        @pl.loop(0, fine)
        def _(f):
            source = f * coarse + side

            @pl.when(source != me)
            def _():
                slot_arrival(source).wait_recv()

            got = arrived[source]
            pieces = [
                split(jnp.where((lane_part == part) & (sub < USED), got, 0.0))
                for part in range(PARTS)
            ]
            stacked[:, pl.ds(pl.multiple_of(f * LANES, LANES), LANES)] = jnp.concatenate(
                [pieces[part][s] for s in range(2) for part in range(PARTS)], axis=0
            ).astype(jnp.bfloat16)

        more = jnp.dot(stacked[...], selector[side], preferred_element_type=jnp.float32)
        sums = more if sums is None else sums + more

    whole = sums[: PARTS * 8, :] + sums[PARTS * 8 :, :]
    for c in range(3):
        load[c * 8 : c * 8 + 5, :] = whole[c * 8 : c * 8 + 5, :]
    load[5:8, :] = whole[24:27, :]
    load[13:15, :] = whole[27:29, :]
    load[15:16, :] = whole[32:33, :]
    load[21:24, :] = whole[33:36, :]


def hand_over(smoothed, load, smoothed_out, load_out, sem):
    pairs = ((smoothed, smoothed_out), (load, load_out))
    copies = [pltpu.make_async_copy(a, b, sem.at[n]) for n, (a, b) in enumerate(pairs)]
    for copy in copies:
        copy.start()
    for copy in copies:
        copy.wait()


def on_device(sizes, force, inv_diag, k_ref, coefs, conn, felem, weights, counts, celem):
    devices = sizes[0] * sizes[1]
    nodes = force.shape[1]
    elems = conn.shape[1]
    slots = felem.shape[0]
    rows = (nodes + 2 * BAND) // ROW
    stride = -(-rows // 8) * 8
    edge_rows = 6 * BAND // ROW
    field = pltpu.VMEM((3 * stride, ROW), jnp.float32)
    edges = pltpu.VMEM((SWEEPS + 1, 2, edge_rows * ROW // LANES, LANES), jnp.float32)
    vmem = pl.BlockSpec(memory_space=pltpu.VMEM)
    hbm = pl.BlockSpec(memory_space=pltpu.HBM)
    given = (force, inv_diag, k_ref, coefs, conn, felem, weights, counts, celem)
    taken = [pltpu.with_memory_space_constraint(v, pltpu.HBM) for v in given]
    outs = pl.pallas_call(
        functools.partial(kernel, sizes),
        out_shape=(
            pltpu.VMEM((3, nodes), jnp.float32),
            pltpu.VMEM((24, CE_DEV), jnp.float32),
        ),
        in_specs=[hbm] * 9,
        out_specs=(vmem, vmem),
        scratch_shapes=[
            pltpu.VMEM((3, nodes), jnp.float32),
            pltpu.VMEM((3, nodes), jnp.float32),
            pltpu.VMEM((24, 24), jnp.float32),
            pltpu.VMEM((1, elems), jnp.float32),
            pltpu.VMEM((8, elems), jnp.int32),
            pltpu.VMEM((1, slots), jnp.int32),
            pltpu.VMEM((8, 8, slots), jnp.float32),
            pltpu.VMEM((1, slots), jnp.int32),
            pltpu.SMEM((1, devices), jnp.int32),
            field,
            field,
            field,
            field,
            pltpu.VMEM((24, elems), jnp.float32),
            pltpu.VMEM((24, elems), jnp.float32),
            pltpu.VMEM((24 * TERMS, elems), jnp.float32),
            pltpu.VMEM((8, elems), jnp.int32),
            pltpu.VMEM((8, elems), jnp.int32),
            pltpu.VMEM((8, ROW, elems), F8),
            pltpu.VMEM((8, elems, ROW), F8),
            pltpu.VMEM((PAD, LANES), jnp.float32),
            pltpu.VMEM((PAD, LANES), jnp.float32),
            pltpu.VMEM((8 * BLOCK, elems - ASIDE * LANES), jnp.bfloat16),
            pltpu.VMEM((48, 8 * BLOCK), jnp.bfloat16),
            pltpu.VMEM((8, slots), jnp.int32),
            pltpu.VMEM((24, GROUP * CAP), jnp.float32),
            pltpu.VMEM((24, slots), jnp.float32),
            pltpu.VMEM((devices, 8, LANES), jnp.float32),
            pltpu.VMEM((sizes[1], sizes[0] * LANES, CE_DEV), jnp.bfloat16),
            pltpu.VMEM((devices, 8, LANES), jnp.float32),
            pltpu.VMEM((2 * PARTS * 8, sizes[0] * LANES), jnp.bfloat16),
            edges,
            edges,
            pltpu.SemaphoreType.DMA((SWEEPS + 1, 2)),
            pltpu.SemaphoreType.DMA((SWEEPS + 1, 2)),
            pltpu.SemaphoreType.DMA((devices,)),
            pltpu.SemaphoreType.DMA((devices,)),
            pltpu.SemaphoreType.DMA((9,)),
        ],
        compiler_params=pltpu.CompilerParams(
            collective_id=0, has_side_effects=True, vmem_limit_bytes=40 * 1024 * 1024
        ),
    )(*taken)
    outs = [pltpu.with_memory_space_constraint(v, pltpu.VMEM) for v in outs]
    return pl.pallas_call(
        hand_over,
        out_shape=(
            jax.ShapeDtypeStruct((3, nodes), jnp.float32),
            jax.ShapeDtypeStruct((24, CE_DEV), jnp.float32),
        ),
        in_specs=[vmem, vmem],
        out_specs=(hbm, hbm),
        scratch_shapes=[pltpu.SemaphoreType.DMA((2,))],
    )(*outs)


def solution(mesh):
    both = ("fine", "coarse")
    placed = (
        P(None, both),
        P(None, both),
        P(),
        P(both),
        P(None, both),
        P(both),
        P(None, None, both),
        P(both, None),
        P(both, None),
    )
    sizes = (mesh.shape["fine"], mesh.shape["coarse"])
    return jax.shard_map(
        functools.partial(on_device, sizes),
        mesh=mesh,
        in_specs=placed,
        out_specs=(P(None, both), P(None, both)),
        check_vma=False,
    )
```
